256 devices in a mesh: seq: 64 (over y, z, x_hi), ch: 4 (over x_lo, core).
Axes of the slice: x: 4 (x_hi: 2, x_lo: 2; x = x_hi * 2 + x_lo), y: 4, z: 8, core: 2. Of those that a mesh axis runs over, the one named last changes fastest.
Arguments:
- value_in: bfloat16 [4096, 8192], P('ch', 'seq'), may hold values from -6 to 6
- gate_inner: bfloat16 [4096, 8192], P('ch', 'seq'), may hold values from -6 to 6
- gate_outer: bfloat16 [4096, 8192], P('ch', 'seq'), may hold values from -6 to 6
- out_grad: bfloat16 [4096, 8192], P('ch', 'seq'), may hold values from -6 to 6
- filter_proj: bfloat16 [2, 4096, 64], P(None, 'ch'), may hold values from -0.75 to 0.75
- decay: float32 [2, 4096], P(None, 'ch'), may hold values from 6.1035156e-05 to 0.05
- frequency: float32 [64], replicated, may hold values from 0.001 to 3
Outputs:
- grad_value: bfloat16 [4096, 8192], P('ch', 'seq')
- grad_gate_inner: bfloat16 [4096, 8192], P('ch', 'seq')
- grad_gate_outer: bfloat16 [4096, 8192], P('ch', 'seq')
- filter_grad: float32 [2, 4096, 64], P(None, 'ch')
The draws below stay inside these ranges and needn't reach their ends.
All inputs are finite; a program needn't handle non-finite values.
Results may differ from the reference program's by a relative error of at most 0.0025.
Values may be sent and summed in bfloat16 or wider, within the bound.
A program may use at most 64 MiB of HBM per device.

```python
import math
import jax
import jax.numpy as jnp
from jax import lax

D = 4096
F = 64
SEQ = 8192


def shard_levels(stream_key, extent, shards, least, top_value):
    def one(axis_at, blocks):
        steps = jax.random.uniform(jax.random.fold_in(jax.random.fold_in(stream_key, 6), axis_at), (blocks,), jnp.float32, least / len(shards), top_value / len(shards))
        return jnp.repeat(jnp.exp(steps), extent[axis_at] // blocks).reshape((-1,) + (1,) * (len(extent) - axis_at - 1))

    factor_of = one(*shards[0])
    for cut in shards[1:]:
        factor_of = factor_of * one(*cut)
    return factor_of


def noise(key, extent, width, bound, cuts=(), held_as=jnp.bfloat16):
    level = shard_levels(key, extent, cuts, -0.22, 0.18) if cuts else 1.0
    array = jax.random.normal(key, extent, jnp.float32) * width * level
    return jnp.minimum(jnp.maximum(array, -bound), bound).astype(held_as)


def setup_inputs(seed: int = 0) -> dict:
    seeds = jax.random.split(jax.random.key(seed), 8)
    return {
        "value_in": noise(seeds[0], (D, SEQ), 1.0, 6.0, ((0, 4), (1, 64))),
        "gate_inner": noise(seeds[1], (D, SEQ), 1.0, 6.0, ((0, 4), (1, 64))),
        "gate_outer": noise(seeds[2], (D, SEQ), 1.0, 6.0, ((0, 4), (1, 64))),
        "out_grad": noise(seeds[3], (D, SEQ), 1.0, 6.0, ((0, 4), (1, 64))),
        "filter_proj": noise(seeds[4], (2, D, F), F ** -0.5, 0.75, ((1, 4),)),
        "decay": jnp.clip(jnp.exp(math.log(0.05) - 6.7083283 * jax.random.uniform(seeds[5], (2, D), jnp.float32) ** shard_levels(seeds[5], (2, D), ((1, 4),), -0.2, 0.2)), 6.103515625e-05, 0.05),
        "frequency": jnp.clip(jnp.exp(jax.random.uniform(seeds[6], (F,), jnp.float32, math.log(0.001), math.log(3.0))), 0.001, 3.0),
    }


def reference(value_in, gate_inner, gate_outer, out_grad, filter_proj, decay, frequency):
    length = SEQ
    highest = lax.Precision.HIGHEST
    positions = jnp.arange(length, dtype=jnp.float32)
    features = jnp.sin(frequency[None, :] * (positions[:, None] + 1.0))
    rows = math.gcd(D, 256)
    blocks = D // rows

    def spectrum(signal):
        return jnp.fft.rfft(signal, n=2 * length, axis=-1)

    def restore(spec):
        return jnp.fft.irfft(spec, n=2 * length, axis=-1)[..., :length].astype(jnp.float32)

    def one_block(items):
        value_blk, inner_blk, outer_blk, grad_blk, proj_blk, rates = items
        value_f = value_blk.astype(jnp.float32)
        inner_f = inner_blk.astype(jnp.float32)
        outer_f = outer_blk.astype(jnp.float32)
        grad_f = grad_blk.astype(jnp.float32)
        window = jnp.sqrt(2.0 * rates)[:, :, None] * jnp.exp(-rates[:, :, None] * positions)
        filters = jnp.einsum('kdf,tf->kdt', proj_blk.astype(jnp.float32), features, precision=highest) * window
        inner_spec = spectrum(filters[0])
        outer_spec = spectrum(filters[1])
        value_spec = spectrum(value_f)
        inner_act = restore(inner_spec * value_spec)
        mixed = inner_f * inner_act
        mixed_spec = spectrum(mixed)
        outer_act = restore(outer_spec * mixed_spec)
        grad_outer = grad_f * outer_act
        grad_spec = spectrum(grad_f * outer_f)
        grad_mixed = restore(jnp.conj(outer_spec) * grad_spec)
        grad_outer_filter = restore(jnp.conj(mixed_spec) * grad_spec)
        grad_inner = grad_mixed * inner_act
        inner_grad_spec = spectrum(grad_mixed * inner_f)
        grad_value = restore(jnp.conj(inner_spec) * inner_grad_spec)
        grad_inner_filter = restore(jnp.conj(value_spec) * inner_grad_spec)
        weighted = jnp.stack([grad_inner_filter, grad_outer_filter]) * window
        proj_grad = jnp.einsum('kdt,tf->kdf', weighted, features, precision=highest)
        return (grad_value.astype(jnp.bfloat16), grad_inner.astype(jnp.bfloat16), grad_outer.astype(jnp.bfloat16), proj_grad)
    items = (value_in.reshape(blocks, rows, length), gate_inner.reshape(blocks, rows, length), gate_outer.reshape(blocks, rows, length), out_grad.reshape(blocks, rows, length), filter_proj.reshape(2, blocks, rows, F).transpose(1, 0, 2, 3), decay.reshape(2, blocks, rows).transpose(1, 0, 2))
    grad_value, grad_inner, grad_outer, proj_grad = lax.map(one_block, items)
    proj_grad = proj_grad.transpose(1, 0, 2, 3).reshape(2, D, F)
    scale = lax.rsqrt(jnp.mean(proj_grad * proj_grad) + 1e-06)
    return (grad_value.reshape(D, length), grad_inner.reshape(D, length), grad_outer.reshape(D, length), proj_grad * scale)
```

```python
import functools
from types import SimpleNamespace

import jax
import jax.numpy as jnp
from jax import lax
from jax.experimental import pallas as pl
from jax.experimental.pallas import tpu as pltpu
from jax.sharding import PartitionSpec as P

MESH = pl.DeviceIdType.MESH
f32, bf16 = jnp.float32, jnp.bfloat16
T = 128
N = 64
CH = 16
G = 8
GROUPS = CH // G
HALF = N // 2
ROWS = N * G
F = 64
NN = (((1,), (0,)), ((), ()))
NT = (((1,), (1,)), ((), ()))


def dg(a, b, dims=NN):
    return lax.dot_general(a, b, dims, preferred_element_type=f32)


def split(x):
    hi = x.astype(bf16)
    return hi, (x - hi.astype(f32)).astype(bf16)


def dot3(a, bh, bl, dims=NN):
    ah, al = split(a)
    return dg(ah, bh, dims) + (dg(al, bh, dims) + dg(ah, bl, dims))


def lanes(shape):
    return lax.broadcasted_iota(jnp.int32, shape, len(shape) - 1)


def rows_iota(shape):
    return lax.broadcasted_iota(jnp.int32, shape, 0)


def prepare(first, proj_ref, decay_ref, freq_ref, s):
    pick = lanes((CH, decay_ref.shape[1])) == rows_iota((CH, decay_ref.shape[1])) + first
    one_hot = pick.astype(f32).astype(bf16)
    low = lanes((T, T)) < F
    freq = jnp.concatenate([freq_ref[...], freq_ref[...]], 1)
    pos = rows_iota((T, T)).astype(f32)
    for which, num in ((0, (T - 1.0) - pos), (1, pos + 2.0)):
        angle = freq * num
        cos, sin = jnp.cos(angle), jnp.sin(angle)
        zero = jnp.zeros_like(cos)
        for half, keep in ((0, low), (1, jnp.logical_not(low))):
            for part, val in ((0, cos), (1, sin)):
                hi, lo = split(jnp.where(keep, val, zero))
                at = (which, pl.ds(half * T, T), pl.ds(part * T, T))
                s.basis_hi[at] = hi
                s.basis_lo[at] = lo
    fh, fl = split(jnp.sin(freq * (pos + 1.0)))
    s.feat_hi[...] = fh
    s.feat_lo[...] = fl
    s.flip[...] = (lanes((T, T)) + rows_iota((T, T)) == T - 1).astype(f32).astype(bf16)
    lane = lanes((CH, T)).astype(f32)
    turn = freq * float(T)
    turn_cos, turn_sin = jnp.cos(turn), jnp.sin(turn)
    for k in (0, 1):
        rate = jnp.sum(jnp.where(pick, decay_ref[pl.ds(k, 1), :], 0.0), axis=1, keepdims=True)
        rate = jnp.broadcast_to(rate, (CH, T))
        gain = jnp.sqrt(2.0 * rate)
        weights = dg(one_hot, proj_ref[k], NT)
        weights = jnp.concatenate([weights, weights], 1)
        window = gain * jnp.exp(-rate * lane)
        head = jnp.where(lanes((CH, T)) < F, weights, 0.0).astype(bf16)
        taps = (dg(head, fh, NT) + dg(head, fl, NT)) * window
        shrink = jnp.exp(-rate * float(T))
        for name, val in (
            ("gain", gain),
            ("weight", weights * gain),
            ("window", window),
            ("taps", taps),
            ("near", jnp.exp(-rate * ((T - 1.0) - lane))),
            ("far", jnp.exp(-rate * (lane + 1.0))),
            ("turn_re", shrink * turn_cos),
            ("turn_im", shrink * turn_sin),
        ):
            getattr(s, name)[k] = val
    ahead = lanes((T, T)) >= rows_iota((T, T))

    def toeplitz(i, _):
        k, d = i // CH, lax.rem(i, CH)
        row = jnp.broadcast_to(s.taps[k, pl.ds(d, 1), :], (T, T))
        mat = jnp.where(ahead, pltpu.roll(row, 0, 1, stride=1, stride_axis=0), 0.0)
        hi, lo = split(mat)
        s.toep_hi[i] = hi
        s.toep_lo[i] = lo
        return 0

    lax.fori_loop(0, 2 * CH, toeplitz, 0, unroll=2)


def of_channel(d):
    return pl.ds(d, N, stride=G)


def group_rows(g):
    return pl.ds(pl.multiple_of(g * G, G), G)


def over_chunks(x, row):
    n, m = x.shape[0] // G, x.shape[1]
    return (x.reshape(n, G, m) * row[None]).reshape(n * G, m)


def modal(x, weight, which, out, s):
    scaled = over_chunks(x, weight)
    scaled = jnp.concatenate([scaled[: ROWS // 2], scaled[ROWS // 2 :]], 1)
    out[...] = dot3(scaled, s.basis_hi[which], s.basis_lo[which])


def scan(src, dst, re, im, backward):
    def at(c):
        c = HALF - 1 - c if backward else c
        return pl.ds(pl.multiple_of(c * G, G), G)

    def step(store, c, carry):
        zr, zi = carry
        rows = at(c)
        if store:
            dst[rows, :T] = zr
            dst[rows, T:] = zi
        return (re * zr - im * zi) + src[rows, :T], (re * zi + im * zr) + src[rows, T:]

    zero = jnp.zeros((G, T), f32)
    end = lax.fori_loop(0, HALF, functools.partial(step, False), (zero, zero), unroll=8)
    late = lanes((G, T)) < F if backward else lanes((G, T)) >= F
    begin = tuple(jnp.where(late, pltpu.roll(x, F, 1), 0.0) for x in end)
    lax.fori_loop(0, HALF, functools.partial(step, True), begin, unroll=8)


def carried(state, weight, decay, which, s):
    z = jnp.concatenate([over_chunks(state[:, T:], weight), over_chunks(state[:, :T], weight)], 1)
    y = dot3(z, s.basis_hi[which], s.basis_lo[which], NT)
    return over_chunks(jnp.concatenate([y[:, :T], y[:, T:]], 0), decay)


def conv(k, g, x, exact, s):
    grow = group_rows(g)
    modal(x[...], s.near[k, grow, :], 0, s.local, s)
    scan(s.local, s.state.at[k], s.turn_re[k, grow, :], s.turn_im[k, grow, :], False)

    def channel(d, _):
        i = k * CH + g * G + d
        xh, xl = split(x[of_channel(d), :])
        y = dg(xh, s.toep_hi[i]) + dg(xh, s.toep_lo[i])
        if not exact:
            y = y + dg(xl, s.toep_hi[i])
        s.y[of_channel(d), :] = y
        return 0

    lax.fori_loop(0, G, channel, 0, unroll=4)
    return s.y[...] + carried(s.state[k], s.weight[k, grow, :], s.far[k, grow, :], 1, s)


def corr(k, g, x, signal, exact, s):
    grow = group_rows(g)
    modal(x[...], s.far[k, grow, :], 1, s.local, s)
    scan(s.local, s.back, s.turn_re[k, grow, :], s.turn_im[k, grow, :], True)

    def channel(d, _):
        i = k * CH + g * G + d
        xh, xl = split(x[of_channel(d), :])
        th = s.toep_hi[i]
        s.y[of_channel(d), :] = dg(xh, th, NT) + dg(xl, th, NT) + dg(xh, s.toep_lo[i], NT)
        vh, vl = split(signal[of_channel(d), :])
        if exact:
            left, right = [vh, vh], [xh, xl]
        else:
            left, right = [vh, vl, vh], [xh, xh, xl]
        turned = dg(s.flip[...], jnp.concatenate(left, 0), NT).astype(bf16)
        pairs = dg(turned, jnp.concatenate(right, 0))
        pairs = pltpu.roll(pairs, 1, 1, stride=1, stride_axis=0)
        pairs = jnp.where(lanes((T, T)) <= rows_iota((T, T)), pairs, 0.0)
        s.lag[pl.ds(d, 1), :] = jnp.sum(pairs, axis=0, keepdims=True)
        return 0

    lax.fori_loop(0, G, channel, 0, unroll=4)
    both = s.local[:, :T] * s.state[k, :, T:] + s.local[:, T:] * s.state[k, :, :T]
    both = jnp.sum(both.reshape(HALF, G, T), axis=0)
    both = both + pltpu.roll(both, F, 1)
    grad = dot3(s.lag[...] * s.window[k, grow, :], s.feat_hi[...], s.feat_lo[...])
    grad = grad + both * s.gain[k, grow, :]
    y = s.y[...] + carried(s.back, s.weight[k, grow, :], s.near[k, grow, :], 0, s)
    return y, grad


def compute_group(g, load, send, s):
    s.v[...] = load(0)
    inner_act = conv(0, g, s.v, True, s)
    s.act[...] = inner_act
    s.mixed[...] = load(1) * inner_act
    outer_act = conv(1, g, s.mixed, False, s)
    out_grad = load(3)
    send(2, out_grad * outer_act)
    s.x[...] = out_grad * load(2)
    grad_mixed, grad_outer = corr(1, g, s.x, s.mixed, False, s)
    send(1, grad_mixed * s.act[...])
    s.x[...] = grad_mixed * load(1)
    grad_value, grad_inner = corr(0, g, s.x, s.v, True, s)
    send(0, grad_value)
    s.own[group_rows(g), :] = jnp.where(lanes((G, T)) < F, grad_inner, grad_outer)


COMPUTE_SCRATCH = dict(
    basis_hi=((2, 2 * T, 2 * T), bf16),
    basis_lo=((2, 2 * T, 2 * T), bf16),
    feat_hi=((T, T), bf16),
    feat_lo=((T, T), bf16),
    flip=((T, T), bf16),
    gain=((2, CH, T), f32),
    weight=((2, CH, T), f32),
    window=((2, CH, T), f32),
    taps=((2, CH, T), f32),
    near=((2, CH, T), f32),
    far=((2, CH, T), f32),
    turn_re=((2, CH, T), f32),
    turn_im=((2, CH, T), f32),
    toep_hi=((2 * CH, T, T), bf16),
    toep_lo=((2 * CH, T, T), bf16),
    local=((ROWS // 2, 2 * T), f32),
    state=((2, ROWS // 2, 2 * T), f32),
    back=((ROWS // 2, 2 * T), f32),
    v=((ROWS, T), f32),
    mixed=((ROWS, T), f32),
    act=((ROWS, T), f32),
    x=((ROWS, T), f32),
    y=((ROWS, T), f32),
    lag=((G, T), f32),
    own=((CH, T), f32),
)


def remote(src, dst, send, recv, **where):
    return pltpu.make_async_remote_copy(
        src_ref=src, dst_ref=dst, send_sem=send, recv_sem=recv, device_id=where, device_id_type=MESH
    )


def await_bytes(ref, sem):
    pltpu.make_async_copy(ref, ref, sem).wait()


def kernel(names, quarter, *refs):
    inputs, refs = refs[:4], refs[4:]
    proj_ref, decay_ref, freq_ref = refs[:3]
    outputs, grad_ref, refs = refs[3:6], refs[6], refs[7:]
    s = SimpleNamespace(**dict(zip(names, refs)))
    me, mine = lax.axis_index("seq"), lax.axis_index("ch")
    mx, mz, my = lax.rem(me, 2), lax.rem(me // 2, 8), me // 16

    barrier = pltpu.get_barrier_semaphore()

    def greet(j, _):
        pl.semaphore_signal(
            barrier, inc=1, device_id={"seq": lax.rem(me + j, N)}, device_id_type=MESH
        )
        return 0

    lax.fori_loop(1, N, greet, 0)
    for j in range(1, quarter):
        pl.semaphore_signal(
            barrier, inc=1, device_id={"ch": lax.rem(mine + j, quarter)}, device_id_type=MESH
        )
    pl.semaphore_wait(barrier, N - 1 + quarter - 1)

    def block_rows(p, g):
        return pl.ds(pl.multiple_of(p * CH + g * G, G), G)

    for g in range(GROUPS):
        for i in (0, 1, 3, 2):

            def push(j, _, g=g, i=i):
                p = lax.rem(me + j, N)
                remote(
                    inputs[i].at[block_rows(p, g), :],
                    s.came.at[i, g, me],
                    s.in_send.at[i, g],
                    s.in_recv.at[i, g],
                    seq=p,
                ).start()
                return 0

            lax.fori_loop(1, N, push, 0)
            pltpu.make_async_copy(
                inputs[i].at[block_rows(me, g), :], s.came.at[i, g, me], s.in_recv.at[i, g]
            ).start()

    prepare(me * CH, proj_ref, decay_ref, freq_ref, s)

    def group(g, _):
        here = set()

        def load(i):
            if i not in here:
                here.add(i)
                await_bytes(s.came.at[i, g], s.in_recv.at[i, g])
            return s.came[i, g].reshape(ROWS, T).astype(f32)

        def send(i, val):
            s.goes[i, g] = val.astype(bf16).reshape(N, G, T)

            def push(j, _):
                p = lax.rem(me + j, N)
                remote(
                    s.goes.at[i, g, p],
                    outputs[i].at[block_rows(me, g), :],
                    s.out_send.at[i, g],
                    s.out_recv.at[i],
                    seq=p,
                ).start()
                return 0

            lax.fori_loop(1, N, push, 0)
            pltpu.make_async_copy(
                s.goes.at[i, g, me], outputs[i].at[block_rows(me, g), :], s.out_recv.at[i]
            ).start()

        compute_group(g, load, send, s)
        return 0

    lax.fori_loop(0, GROUPS, group, 0)

    s.every[mx, my, mz] = s.own[...]
    for j in range(1, 8):
        z = lax.rem(mz + j, 8)
        spot = s.every.at[mx, my, mz]
        remote(spot, spot, s.share_send.at[0], s.share_recv.at[0], seq=my * 16 + z * 2 + mx).start()
    await_bytes(s.every.at[0, 0, pl.ds(0, 7)], s.share_recv.at[0])
    for j in range(1, 4):
        y = lax.rem(my + j, 4)
        spot = s.every.at[mx, my]
        remote(spot, spot, s.share_send.at[1], s.share_recv.at[1], seq=y * 16 + mz * 2 + mx).start()
    await_bytes(s.every.at[0, pl.ds(0, 3)], s.share_recv.at[1])
    spot = s.every.at[mx]
    remote(spot, spot, s.share_send.at[2], s.share_recv.at[2], seq=my * 16 + mz * 2 + 1 - mx).start()
    await_bytes(s.every.at[0], s.share_recv.at[2])

    grads = s.every[...]
    square = jnp.sum((grads * grads).reshape(N * CH // 8, 8, T), axis=0)
    s.square[mine] = square
    for j in range(1, quarter):
        spot = s.square.at[mine]
        remote(
            spot, spot, s.share_send.at[3], s.share_recv.at[3], ch=lax.rem(mine + j, quarter)
        ).start()
    await_bytes(s.square.at[pl.ds(0, quarter - 1)], s.share_recv.at[3])
    total = jnp.sum(s.square[...], axis=(0, 1), keepdims=True)[0]
    total = jnp.sum(total, axis=1, keepdims=True)
    scale = lax.rsqrt(total / float(2 * F * CH * N * quarter) + 1e-06)
    for y in range(4):
        for z in range(8):
            for x in range(2):
                p = y * 16 + z * 2 + x
                grad_ref[pl.ds(p * CH, CH), :] = s.every[x, y, z] * scale

    for i in range(3):
        await_bytes(outputs[i], s.out_recv.at[i])
    for g in range(GROUPS):
        for i in range(4):
            await_bytes(s.came.at[i, g, pl.ds(0, N - 1)], s.in_send.at[i, g])
        for i in range(3):
            await_bytes(s.goes.at[i, g, pl.ds(0, N - 1)], s.out_send.at[i, g])
    await_bytes(s.every.at[0, 0, pl.ds(0, 7)], s.share_send.at[0])
    await_bytes(s.every.at[0, pl.ds(0, 3)], s.share_send.at[1])
    await_bytes(s.every.at[0], s.share_send.at[2])
    await_bytes(s.square.at[pl.ds(0, quarter - 1)], s.share_send.at[3])


def body(quarter, value_in, gate_inner, gate_outer, out_grad, filter_proj, decay, frequency):
    scratch = {name: pltpu.VMEM(*spec) for name, spec in COMPUTE_SCRATCH.items()}
    scratch |= dict(
        came=pltpu.VMEM((4, GROUPS, N, G, T), bf16),
        goes=pltpu.VMEM((3, GROUPS, N, G, T), bf16),
        every=pltpu.VMEM((2, 4, 8, CH, T), f32),
        square=pltpu.VMEM((quarter, 8, T), f32),
        in_send=pltpu.SemaphoreType.DMA((4, GROUPS)),
        in_recv=pltpu.SemaphoreType.DMA((4, GROUPS)),
        out_send=pltpu.SemaphoreType.DMA((3, GROUPS)),
        out_recv=pltpu.SemaphoreType.DMA((3,)),
        share_send=pltpu.SemaphoreType.DMA((4,)),
        share_recv=pltpu.SemaphoreType.DMA((4,)),
    )
    local = jax.ShapeDtypeStruct(value_in.shape, bf16)
    anywhere, vmem = pl.BlockSpec(memory_space=pl.ANY), pl.BlockSpec(memory_space=pltpu.VMEM)
    grad_value, grad_inner, grad_outer, grads = pl.pallas_call(
        functools.partial(kernel, tuple(scratch), quarter),
        out_shape=(local, local, local, jax.ShapeDtypeStruct((N * CH, T), f32)),
        in_specs=[anywhere] * 4 + [vmem] * 3,
        out_specs=[anywhere] * 3 + [vmem],
        scratch_shapes=list(scratch.values()),
        compiler_params=pltpu.CompilerParams(
            collective_id=0, has_side_effects=True, vmem_limit_bytes=40 << 20
        ),
    )(
        value_in,
        gate_inner,
        gate_outer,
        out_grad,
        jnp.transpose(filter_proj, (0, 2, 1)),
        decay,
        frequency.reshape(1, F),
    )
    filter_grad = jnp.transpose(grads.reshape(N * CH, 2, F), (1, 0, 2))
    return grad_value, grad_inner, grad_outer, filter_grad


def solution(mesh):
    placed = (P("ch", "seq"),) * 4 + (P(None, "ch", None), P(None, "ch"), P())
    return jax.shard_map(
        functools.partial(body, mesh.shape["ch"]),
        mesh=mesh,
        in_specs=placed,
        out_specs=(P("ch", "seq"),) * 3 + (P(None, "ch", None),),
        check_vma=False,
    )
```

```python
import functools
from types import SimpleNamespace

import jax
import jax.numpy as jnp
from jax import lax
from jax.experimental import pallas as pl
from jax.experimental.pallas import tpu as pltpu
from jax.sharding import PartitionSpec as P

MESH = pl.DeviceIdType.MESH
f32, bf16 = jnp.float32, jnp.bfloat16
T = 128
N = 64
CH = 16
G = 8
GROUPS = CH // G
HALF = N // 2
ROWS = N * G
F = 64
NN = (((1,), (0,)), ((), ()))
NT = (((1,), (1,)), ((), ()))


def dg(a, b, dims=NN):
    return lax.dot_general(a, b, dims, preferred_element_type=f32)


def split(x):
    hi = x.astype(bf16)
    return hi, (x - hi.astype(f32)).astype(bf16)


def dot3(a, bh, bl, dims=NN):
    ah, al = split(a)
    return dg(ah, bh, dims) + (dg(al, bh, dims) + dg(ah, bl, dims))


def lanes(shape):
    return lax.broadcasted_iota(jnp.int32, shape, len(shape) - 1)


def rows_iota(shape):
    return lax.broadcasted_iota(jnp.int32, shape, 0)


def prepare(first, proj_ref, decay_ref, freq_ref, s):
    pick = lanes((CH, decay_ref.shape[1])) == rows_iota((CH, decay_ref.shape[1])) + first
    one_hot = pick.astype(f32).astype(bf16)
    low = lanes((T, T)) < F
    freq = jnp.concatenate([freq_ref[...], freq_ref[...]], 1)
    pos = rows_iota((T, T)).astype(f32)
    for which, num in ((0, (T - 1.0) - pos), (1, pos + 2.0)):
        angle = freq * num
        cos, sin = jnp.cos(angle), jnp.sin(angle)
        zero = jnp.zeros_like(cos)
        for half, keep in ((0, low), (1, jnp.logical_not(low))):
            for part, val in ((0, cos), (1, sin)):
                hi, lo = split(jnp.where(keep, val, zero))
                at = (which, pl.ds(half * T, T), pl.ds(part * T, T))
                s.basis_hi[at] = hi
                s.basis_lo[at] = lo
    fh, fl = split(jnp.sin(freq * (pos + 1.0)))
    s.feat_hi[...] = fh
    s.feat_lo[...] = fl
    s.flip[...] = (lanes((T, T)) + rows_iota((T, T)) == T - 1).astype(f32).astype(bf16)
    lane = lanes((CH, T)).astype(f32)
    turn = freq * float(T)
    turn_cos, turn_sin = jnp.cos(turn), jnp.sin(turn)
    for k in (0, 1):
        rate = jnp.sum(jnp.where(pick, decay_ref[pl.ds(k, 1), :], 0.0), axis=1, keepdims=True)
        rate = jnp.broadcast_to(rate, (CH, T))
        gain = jnp.sqrt(2.0 * rate)
        weights = dg(one_hot, proj_ref[k], NT)
        weights = jnp.concatenate([weights, weights], 1)
        window = gain * jnp.exp(-rate * lane)
        head = jnp.where(lanes((CH, T)) < F, weights, 0.0).astype(bf16)
        taps = (dg(head, fh, NT) + dg(head, fl, NT)) * window
        shrink = jnp.exp(-rate * float(T))
        for name, val in (
            ("gain", gain),
            ("weight", weights * gain),
            ("window", window),
            ("taps", taps),
            ("near", jnp.exp(-rate * ((T - 1.0) - lane))),
            ("far", jnp.exp(-rate * (lane + 1.0))),
            ("turn_re", shrink * turn_cos),
            ("turn_im", shrink * turn_sin),
        ):
            getattr(s, name)[k] = val
    ahead = lanes((T, T)) >= rows_iota((T, T))

    def toeplitz(i, _):
        k, d = i // CH, lax.rem(i, CH)
        row = jnp.broadcast_to(s.taps[k, pl.ds(d, 1), :], (T, T))
        mat = jnp.where(ahead, pltpu.roll(row, 0, 1, stride=1, stride_axis=0), 0.0)
        hi, lo = split(mat)
        s.toep_hi[i] = hi
        s.toep_lo[i] = lo
        return 0

    lax.fori_loop(0, 2 * CH, toeplitz, 0, unroll=2)


def of_channel(d):
    return pl.ds(d, N, stride=G)


def group_rows(g):
    return pl.ds(pl.multiple_of(g * G, G), G)


def over_chunks(x, row):
    n, m = x.shape[0] // G, x.shape[1]
    return (x.reshape(n, G, m) * row[None]).reshape(n * G, m)


def modal(x, weight, which, out, s):
    scaled = over_chunks(x, weight)
    scaled = jnp.concatenate([scaled[: ROWS // 2], scaled[ROWS // 2 :]], 1)
    out[...] = dot3(scaled, s.basis_hi[which], s.basis_lo[which])


def scan(src, dst, re, im, backward):
    def at(c):
        c = HALF - 1 - c if backward else c
        return pl.ds(pl.multiple_of(c * G, G), G)

    def step(store, c, carry):
        zr, zi = carry
        rows = at(c)
        if store:
            dst[rows, :T] = zr
            dst[rows, T:] = zi
        return (re * zr - im * zi) + src[rows, :T], (re * zi + im * zr) + src[rows, T:]

    zero = jnp.zeros((G, T), f32)
    end = lax.fori_loop(0, HALF, functools.partial(step, False), (zero, zero), unroll=8)
    late = lanes((G, T)) < F if backward else lanes((G, T)) >= F
    begin = tuple(jnp.where(late, pltpu.roll(x, F, 1), 0.0) for x in end)
    lax.fori_loop(0, HALF, functools.partial(step, True), begin, unroll=8)


def carried(state, weight, decay, which, s):
    z = jnp.concatenate([over_chunks(state[:, T:], weight), over_chunks(state[:, :T], weight)], 1)
    y = dot3(z, s.basis_hi[which], s.basis_lo[which], NT)
    return over_chunks(jnp.concatenate([y[:, :T], y[:, T:]], 0), decay)


def conv(k, g, x, exact, s):
    grow = group_rows(g)
    modal(x[...], s.near[k, grow, :], 0, s.local, s)
    scan(s.local, s.state.at[k], s.turn_re[k, grow, :], s.turn_im[k, grow, :], False)

    def channel(d, _):
        i = k * CH + g * G + d
        xh, xl = split(x[of_channel(d), :])
        y = dg(xh, s.toep_hi[i]) + dg(xh, s.toep_lo[i])
        if not exact:
            y = y + dg(xl, s.toep_hi[i])
        s.y[of_channel(d), :] = y
        return 0

    lax.fori_loop(0, G, channel, 0, unroll=4)
    return s.y[...] + carried(s.state[k], s.weight[k, grow, :], s.far[k, grow, :], 1, s)


def corr(k, g, x, signal, exact, s):
    grow = group_rows(g)
    modal(x[...], s.far[k, grow, :], 1, s.local, s)
    scan(s.local, s.back, s.turn_re[k, grow, :], s.turn_im[k, grow, :], True)

    def channel(d, _):
        i = k * CH + g * G + d
        xh, xl = split(x[of_channel(d), :])
        th = s.toep_hi[i]
        s.y[of_channel(d), :] = dg(xh, th, NT) + dg(xl, th, NT) + dg(xh, s.toep_lo[i], NT)
        vh, vl = split(signal[of_channel(d), :])
        if exact:
            left, right = [vh, vh], [xh, xl]
        else:
            left, right = [vh, vl, vh], [xh, xh, xl]
        turned = dg(s.flip[...], jnp.concatenate(left, 0), NT).astype(bf16)
        pairs = dg(turned, jnp.concatenate(right, 0))
        pairs = pltpu.roll(pairs, 1, 1, stride=1, stride_axis=0)
        pairs = jnp.where(lanes((T, T)) <= rows_iota((T, T)), pairs, 0.0)
        s.lag[pl.ds(d, 1), :] = jnp.sum(pairs, axis=0, keepdims=True)
        return 0

    lax.fori_loop(0, G, channel, 0, unroll=4)
    both = s.local[:, :T] * s.state[k, :, T:] + s.local[:, T:] * s.state[k, :, :T]
    both = jnp.sum(both.reshape(HALF, G, T), axis=0)
    both = both + pltpu.roll(both, F, 1)
    grad = dot3(s.lag[...] * s.window[k, grow, :], s.feat_hi[...], s.feat_lo[...])
    grad = grad + both * s.gain[k, grow, :]
    y = s.y[...] + carried(s.back, s.weight[k, grow, :], s.near[k, grow, :], 0, s)
    return y, grad


def compute_group(g, load, send, s):
    s.v[...] = load(0)
    inner_act = conv(0, g, s.v, True, s)
    s.act[...] = inner_act
    s.mixed[...] = load(1) * inner_act
    outer_act = conv(1, g, s.mixed, False, s)
    out_grad = load(3)
    send(2, out_grad * outer_act)
    s.x[...] = out_grad * load(2)
    grad_mixed, grad_outer = corr(1, g, s.x, s.mixed, False, s)
    send(1, grad_mixed * s.act[...])
    s.x[...] = grad_mixed * load(1)
    grad_value, grad_inner = corr(0, g, s.x, s.v, True, s)
    send(0, grad_value)
    return jnp.where(lanes((G, T)) < F, grad_inner, grad_outer)


COMPUTE_SCRATCH = dict(
    basis_hi=((2, 2 * T, 2 * T), bf16),
    basis_lo=((2, 2 * T, 2 * T), bf16),
    feat_hi=((T, T), bf16),
    feat_lo=((T, T), bf16),
    flip=((T, T), bf16),
    gain=((2, CH, T), f32),
    weight=((2, CH, T), f32),
    window=((2, CH, T), f32),
    taps=((2, CH, T), f32),
    near=((2, CH, T), f32),
    far=((2, CH, T), f32),
    turn_re=((2, CH, T), f32),
    turn_im=((2, CH, T), f32),
    toep_hi=((2 * CH, T, T), bf16),
    toep_lo=((2 * CH, T, T), bf16),
    local=((ROWS // 2, 2 * T), f32),
    state=((2, ROWS // 2, 2 * T), f32),
    back=((ROWS // 2, 2 * T), f32),
    v=((ROWS, T), f32),
    mixed=((ROWS, T), f32),
    act=((ROWS, T), f32),
    x=((ROWS, T), f32),
    y=((ROWS, T), f32),
    lag=((G, T), f32),
)


def remote(src, dst, send, recv, **where):
    return pltpu.make_async_remote_copy(
        src_ref=src, dst_ref=dst, send_sem=send, recv_sem=recv, device_id=where, device_id_type=MESH
    )


def await_bytes(ref, sem):
    pltpu.make_async_copy(ref, ref, sem).wait()


def kernel(names, quarter, *refs):
    inputs, refs = refs[:4], refs[4:]
    small = refs[:3]
    outputs, grad_ref, refs = refs[3:6], refs[6], refs[7:]
    s = SimpleNamespace(**dict(zip(names, refs)))
    me, mine = lax.axis_index("seq"), lax.axis_index("ch")
    mx, mz, my = lax.rem(me, 2), lax.rem(me // 2, 8), me // 16

    tables = (s.proj, s.decay, s.freq)
    for i in range(3):
        pltpu.make_async_copy(small[i], tables[i], s.table_sem.at[i]).start()
    barrier = pltpu.get_barrier_semaphore()

    def greet(j, _):
        pl.semaphore_signal(
            barrier, inc=1, device_id={"seq": lax.rem(me + j, N)}, device_id_type=MESH
        )
        return 0

    def layer(j):
        return dict(seq=lax.rem(j, 4) * 16 + mz * 2 + lax.rem(j // 4, 2), ch=j // 8)

    def greet_layer(j, _):
        spot = layer(lax.rem(mine * 8 + j, layer_size))
        pl.semaphore_signal(barrier, inc=1, device_id=spot, device_id_type=MESH)
        return 0

    layer_size = 8 * quarter
    lax.fori_loop(1, N, greet, 0, unroll=9)
    lax.fori_loop(8, layer_size, greet_layer, 0, unroll=8)
    pl.semaphore_wait(barrier, N - 1 + layer_size - 8)

    def block_rows(p, g):
        return pl.ds(pl.multiple_of(p * CH + g * G, G), G)

    for g in range(GROUPS):
        if g == 1:
            for i in range(3):
                pltpu.make_async_copy(small[i], tables[i], s.table_sem.at[i]).wait()
            prepare(me * CH, *tables, s)
        for i in (0, 1, 3, 2):

            def push(j, _, g=g, i=i):
                p = lax.rem(me + j, N)
                remote(
                    inputs[i].at[block_rows(p, g), :],
                    s.came.at[i, g, me],
                    s.in_send.at[i, g],
                    s.in_recv.at[i, g],
                    seq=p,
                ).start()
                return 0

            lax.fori_loop(1, N, push, 0, unroll=9)
            pltpu.make_async_copy(
                inputs[i].at[block_rows(me, g), :], s.came.at[i, g, me], s.in_recv.at[i, g]
            ).start()

    def push_out(i, g):
        def push(j, _):
            p = lax.rem(me + j, N)
            remote(
                s.goes.at[i, g, p],
                outputs[i].at[block_rows(me, g), :],
                s.out_send.at[i, g],
                s.out_recv.at[i],
                seq=p,
            ).start()
            return 0

        lax.fori_loop(1, N, push, 0, unroll=9)
        pltpu.make_async_copy(
            s.goes.at[i, g, me], outputs[i].at[block_rows(me, g), :], s.out_recv.at[i]
        ).start()

    def share_column(g):
        spot = s.every.at[g, mx * 4 + my, mz]
        for j in range(1, 8):
            seq = my * 16 + lax.rem(mz + j, 8) * 2 + mx
            remote(spot, spot, s.share_send.at[0, g], s.share_recv.at[0, g], seq=seq).start()

    def share_layer(g):
        await_bytes(s.every.at[g, 0, pl.ds(0, 7)], s.share_recv.at[0, g])
        spot = s.every.at[g, mx * 4 + my]
        for j in range(1, 8):
            seq = layer(lax.rem(mx * 4 + my + j, 8))["seq"]
            remote(spot, spot, s.share_send.at[1, g], s.share_recv.at[1, g], seq=seq).start()

    for g in range(GROUPS):
        last = g == GROUPS - 1
        here = set()

        def load(i, g=g, here=here):
            if i not in here:
                here.add(i)
                await_bytes(s.came.at[i, g], s.in_recv.at[i, g])
            return s.came[i, g].reshape(ROWS, T).astype(f32)

        def send(i, val, g=g, last=last):
            s.goes[i, g] = val.astype(bf16).reshape(N, G, T)
            if not last or i == 2:
                push_out(i, g)

        s.every[g, mx * 4 + my, mz] = compute_group(g, load, send, s)
        share_column(g)
    share_layer(0)
    push_out(1, g)
    push_out(0, g)
    share_layer(g)
    column = s.every[:, mx * 4 + my].reshape(2 * 8 * G, T)
    at = mine * 8 + mx * 4 + my
    s.square[at] = jnp.sum(column * column, axis=0, keepdims=True)

    def push_square(j, _):
        spot = s.square.at[at]
        where = layer(lax.rem(at + j, layer_size))
        remote(spot, spot, s.square_send, s.square_recv, **where).start()
        return 0

    lax.fori_loop(1, layer_size, push_square, 0)

    await_bytes(s.square.at[pl.ds(0, layer_size - 1)], s.square_recv)
    total = jnp.sum(jnp.sum(s.square[...], axis=0), axis=1, keepdims=True)
    scale = lax.rsqrt(total / float(2 * F * CH * N * quarter) + 1e-06)
    for g in range(GROUPS):
        await_bytes(s.every.at[g, pl.ds(0, 7)], s.share_recv.at[1, g])
    for y in range(4):
        for z in range(8):
            for x in range(2):
                for g in range(GROUPS):
                    rows = pl.ds((y * 16 + z * 2 + x) * CH + g * G, G)
                    s.sorted[rows, :] = s.every[g, x * 4 + y, z] * scale
    for j in range(N * CH // T):
        grad_ref[:, pl.ds(j * T, T)] = s.sorted[pl.ds(j * T, T), :].T

    for i in range(3):
        await_bytes(outputs[i], s.out_recv.at[i])
    for g in range(GROUPS):
        for i in range(4):
            await_bytes(s.came.at[i, g, pl.ds(0, N - 1)], s.in_send.at[i, g])
        for i in range(3):
            await_bytes(s.goes.at[i, g, pl.ds(0, N - 1)], s.out_send.at[i, g])
        await_bytes(s.every.at[g, 0, pl.ds(0, 7)], s.share_send.at[0, g])
        await_bytes(s.every.at[g, pl.ds(0, 7)], s.share_send.at[1, g])
    await_bytes(s.square.at[pl.ds(0, layer_size - 1)], s.square_send)


def hand_over(*refs):
    copies = [pltpu.make_async_copy(refs[i], refs[4 + i], refs[8].at[i]) for i in range(4)]
    for copy in copies:
        copy.start()
    for copy in copies:
        copy.wait()


def body(quarter, value_in, gate_inner, gate_outer, out_grad, filter_proj, decay, frequency):
    scratch = {name: pltpu.VMEM(*spec) for name, spec in COMPUTE_SCRATCH.items()}
    scratch |= dict(
        came=pltpu.VMEM((4, GROUPS, N, G, T), bf16),
        goes=pltpu.VMEM((3, GROUPS, N, G, T), bf16),
        every=pltpu.VMEM((GROUPS, 8, 8, G, T), f32),
        sorted=pltpu.VMEM((N * CH, T), f32),
        square=pltpu.VMEM((8 * quarter, 1, T), f32),
        proj=pltpu.VMEM((2, F, filter_proj.shape[1]), bf16),
        decay=pltpu.VMEM(decay.shape, f32),
        freq=pltpu.VMEM((1, F), f32),
        table_sem=pltpu.SemaphoreType.DMA((3,)),
        in_send=pltpu.SemaphoreType.DMA((4, GROUPS)),
        in_recv=pltpu.SemaphoreType.DMA((4, GROUPS)),
        out_send=pltpu.SemaphoreType.DMA((3, GROUPS)),
        out_recv=pltpu.SemaphoreType.DMA((3,)),
        share_send=pltpu.SemaphoreType.DMA((2, GROUPS)),
        share_recv=pltpu.SemaphoreType.DMA((2, GROUPS)),
        square_send=pltpu.SemaphoreType.DMA,
        square_recv=pltpu.SemaphoreType.DMA,
    )
    local = jax.ShapeDtypeStruct(value_in.shape, bf16)
    anywhere, vmem = pl.BlockSpec(memory_space=pl.ANY), pl.BlockSpec(memory_space=pltpu.VMEM)
    hbm = pl.BlockSpec(memory_space=pltpu.HBM)
    results = pl.pallas_call(
        functools.partial(kernel, tuple(scratch), quarter),
        out_shape=(local, local, local, jax.ShapeDtypeStruct((T, N * CH), f32)),
        in_specs=[hbm] * 7,
        out_specs=[anywhere] * 3 + [vmem],
        scratch_shapes=list(scratch.values()),
        compiler_params=pltpu.CompilerParams(
            collective_id=0, has_side_effects=True, vmem_limit_bytes=40 << 20
        ),
    )(
        *(
            pltpu.with_memory_space_constraint(x, pltpu.HBM)
            for x in (
                value_in,
                gate_inner,
                gate_outer,
                out_grad,
                jnp.transpose(filter_proj, (0, 2, 1)),
                decay,
                frequency.reshape(1, F),
            )
        )
    )
    grad_value, grad_inner, grad_outer, grads = pl.pallas_call(
        hand_over,
        out_shape=tuple(jax.ShapeDtypeStruct(x.shape, x.dtype) for x in results),
        in_specs=[vmem] * 4,
        out_specs=[hbm] * 4,
        scratch_shapes=[pltpu.SemaphoreType.DMA((4,))],
    )(*(pltpu.with_memory_space_constraint(x, pltpu.VMEM) for x in results))
    filter_grad = jnp.transpose(grads.reshape(2, F, N * CH), (0, 2, 1))
    return grad_value, grad_inner, grad_outer, filter_grad


def solution(mesh):
    placed = (P("ch", "seq"),) * 4 + (P(None, "ch", None), P(None, "ch"), P())
    return jax.shard_map(
        functools.partial(body, mesh.shape["ch"]),
        mesh=mesh,
        in_specs=placed,
        out_specs=(P("ch", "seq"),) * 3 + (P(None, "ch", None),),
        check_vma=False,
    )
```

```python
import functools
from types import SimpleNamespace

import jax
import jax.numpy as jnp
from jax import lax
from jax.experimental import pallas as pl
from jax.experimental.pallas import tpu as pltpu
from jax.sharding import PartitionSpec as P

MESH = pl.DeviceIdType.MESH
f32, bf16 = jnp.float32, jnp.bfloat16
T = 128
N = 64
CH = 16
G = 8
GROUPS = CH // G
HALF = N // 2
ROWS = N * G
F = 64
NN = (((1,), (0,)), ((), ()))
NT = (((1,), (1,)), ((), ()))


def dg(a, b, dims=NN):
    return lax.dot_general(a, b, dims, preferred_element_type=f32)


def split(x):
    hi = x.astype(bf16)
    return hi, (x - hi.astype(f32)).astype(bf16)


def dot3(a, bh, bl, dims=NN):
    ah, al = split(a)
    return dg(ah, bh, dims) + (dg(al, bh, dims) + dg(ah, bl, dims))


def lanes(shape):
    return lax.broadcasted_iota(jnp.int32, shape, len(shape) - 1)


def rows_iota(shape):
    return lax.broadcasted_iota(jnp.int32, shape, 0)


def prepare(first, proj_ref, decay_ref, freq_ref, s):
    pick = lanes((CH, decay_ref.shape[1])) == rows_iota((CH, decay_ref.shape[1])) + first
    one_hot = pick.astype(f32).astype(bf16)
    low = lanes((T, T)) < F
    freq = jnp.concatenate([freq_ref[...], freq_ref[...]], 1)
    pos = rows_iota((T, T)).astype(f32)
    for which, num in ((0, (T - 1.0) - pos), (1, pos + 2.0)):
        angle = freq * num
        cos, sin = jnp.cos(angle), jnp.sin(angle)
        zero = jnp.zeros_like(cos)
        for half, keep in ((0, low), (1, jnp.logical_not(low))):
            for part, val in ((0, cos), (1, sin)):
                hi, lo = split(jnp.where(keep, val, zero))
                at = (which, pl.ds(half * T, T), pl.ds(part * T, T))
                s.basis_hi[at] = hi
                s.basis_lo[at] = lo
    fh, fl = split(jnp.sin(freq * (pos + 1.0)))
    s.feat_hi[...] = fh
    s.feat_lo[...] = fl
    s.flip[...] = (lanes((T, T)) + rows_iota((T, T)) == T - 1).astype(f32).astype(bf16)
    lane = lanes((CH, T)).astype(f32)
    turn = freq * float(T)
    turn_cos, turn_sin = jnp.cos(turn), jnp.sin(turn)
    for k in (0, 1):
        rate = jnp.sum(jnp.where(pick, decay_ref[pl.ds(k, 1), :], 0.0), axis=1, keepdims=True)
        rate = jnp.broadcast_to(rate, (CH, T))
        gain = jnp.sqrt(2.0 * rate)
        weights = dg(one_hot, proj_ref[k], NT)
        weights = jnp.concatenate([weights, weights], 1)
        window = gain * jnp.exp(-rate * lane)
        head = jnp.where(lanes((CH, T)) < F, weights, 0.0).astype(bf16)
        taps = (dg(head, fh, NT) + dg(head, fl, NT)) * window
        shrink = jnp.exp(-rate * float(T))
        for name, val in (
            ("gain", gain),
            ("weight", weights * gain),
            ("window", window),
            ("taps", taps),
            ("near", jnp.exp(-rate * ((T - 1.0) - lane))),
            ("far", jnp.exp(-rate * (lane + 1.0))),
            ("turn_re", shrink * turn_cos),
            ("turn_im", shrink * turn_sin),
        ):
            getattr(s, name)[k] = val
    ahead = lanes((T, T)) >= rows_iota((T, T))

    def toeplitz(i, _):
        k, d = i // CH, lax.rem(i, CH)
        row = jnp.broadcast_to(s.taps[k, pl.ds(d, 1), :], (T, T))
        mat = jnp.where(ahead, pltpu.roll(row, 0, 1, stride=1, stride_axis=0), 0.0)
        hi, lo = split(mat)
        s.toep_hi[i] = hi
        s.toep_lo[i] = lo
        return 0

    lax.fori_loop(0, 2 * CH, toeplitz, 0, unroll=2)


def encode(x):
    top = jnp.maximum(jnp.max(jnp.abs(x), axis=-1, keepdims=True), 1e-35)
    u = x / top
    q = u * u
    q = (q * q) * 2.0**60
    q = q * q
    return jnp.where(u < 0.0, -q, q).astype(bf16), top


def decode(y, top):
    y = y.astype(f32)
    root = jnp.sqrt(jnp.sqrt(jnp.sqrt(jnp.abs(y)) * 2.0**-60))
    root = jnp.where(y < 0.0, -root, jnp.where(y > 0.0, root, 0.0))
    return root * top


def to_lanes(top, first):
    n, m, _ = top.shape
    spot = lax.broadcasted_iota(jnp.int32, (n, m, T), 2) == first + lax.broadcasted_iota(
        jnp.int32, (n, m, T), 1
    )
    return jnp.sum(jnp.where(spot, jnp.broadcast_to(top, (n, m, T)), 0.0), axis=1, keepdims=True)


def from_lanes(row, first, m):
    n = row.shape[0]
    spot = lax.broadcasted_iota(jnp.int32, (n, m, T), 2) == first + lax.broadcasted_iota(
        jnp.int32, (n, m, T), 1
    )
    return jnp.sum(jnp.where(spot, jnp.broadcast_to(row, (n, m, T)), 0.0), axis=2, keepdims=True)


def of_channel(d):
    return pl.ds(d, N, stride=G)


def group_rows(g):
    return pl.ds(pl.multiple_of(g * G, G), G)


def over_chunks(x, row):
    n, m = x.shape[0] // G, x.shape[1]
    return (x.reshape(n, G, m) * row[None]).reshape(n * G, m)


def modal(x, weight, which, out, s):
    scaled = over_chunks(x, weight)
    scaled = jnp.concatenate([scaled[: ROWS // 2], scaled[ROWS // 2 :]], 1)
    out[...] = dot3(scaled, s.basis_hi[which], s.basis_lo[which])


def scan(src, dst, re, im, backward):
    def at(c):
        c = HALF - 1 - c if backward else c
        return pl.ds(pl.multiple_of(c * G, G), G)

    def step(store, c, carry):
        zr, zi = carry
        rows = at(c)
        if store:
            dst[rows, :T] = zr
            dst[rows, T:] = zi
        return (re * zr - im * zi) + src[rows, :T], (re * zi + im * zr) + src[rows, T:]

    zero = jnp.zeros((G, T), f32)
    end = lax.fori_loop(0, HALF, functools.partial(step, False), (zero, zero), unroll=8)
    late = lanes((G, T)) < F if backward else lanes((G, T)) >= F
    begin = tuple(jnp.where(late, pltpu.roll(x, F, 1), 0.0) for x in end)
    lax.fori_loop(0, HALF, functools.partial(step, True), begin, unroll=8)


def carried(state, weight, decay, which, s):
    z = jnp.concatenate([over_chunks(state[:, T:], weight), over_chunks(state[:, :T], weight)], 1)
    y = dot3(z, s.basis_hi[which], s.basis_lo[which], NT)
    return over_chunks(jnp.concatenate([y[:, :T], y[:, T:]], 0), decay)


def conv(k, g, x, exact, s):
    grow = group_rows(g)
    modal(x[...], s.near[k, grow, :], 0, s.local, s)
    scan(s.local, s.state.at[k], s.turn_re[k, grow, :], s.turn_im[k, grow, :], False)

    def channel(d, _):
        i = k * CH + g * G + d
        xh, xl = split(x[of_channel(d), :])
        y = dg(xh, s.toep_hi[i]) + dg(xh, s.toep_lo[i])
        if not exact:
            y = y + dg(xl, s.toep_hi[i])
        s.y[of_channel(d), :] = y
        return 0

    lax.fori_loop(0, G, channel, 0, unroll=4)
    return s.y[...] + carried(s.state[k], s.weight[k, grow, :], s.far[k, grow, :], 1, s)


def corr(k, g, x, signal, exact, s):
    grow = group_rows(g)
    modal(x[...], s.far[k, grow, :], 1, s.local, s)
    scan(s.local, s.back, s.turn_re[k, grow, :], s.turn_im[k, grow, :], True)

    def channel(d, _):
        i = k * CH + g * G + d
        xh, xl = split(x[of_channel(d), :])
        th = s.toep_hi[i]
        s.y[of_channel(d), :] = dg(xh, th, NT) + dg(xl, th, NT) + dg(xh, s.toep_lo[i], NT)
        vh, vl = split(signal[of_channel(d), :])
        if exact:
            left, right = [vh, vh], [xh, xl]
        else:
            left, right = [vh, vl, vh], [xh, xh, xl]
        turned = dg(s.flip[...], jnp.concatenate(left, 0), NT).astype(bf16)
        pairs = dg(turned, jnp.concatenate(right, 0))
        pairs = pltpu.roll(pairs, 1, 1, stride=1, stride_axis=0)
        pairs = jnp.where(lanes((T, T)) <= rows_iota((T, T)), pairs, 0.0)
        s.lag[pl.ds(d, 1), :] = jnp.sum(pairs, axis=0, keepdims=True)
        return 0

    lax.fori_loop(0, G, channel, 0, unroll=4)
    both = s.local[:, :T] * s.state[k, :, T:] + s.local[:, T:] * s.state[k, :, :T]
    both = jnp.sum(both.reshape(HALF, G, T), axis=0)
    both = both + pltpu.roll(both, F, 1)
    grad = dot3(s.lag[...] * s.window[k, grow, :], s.feat_hi[...], s.feat_lo[...])
    grad = grad + both * s.gain[k, grow, :]
    y = s.y[...] + carried(s.back, s.weight[k, grow, :], s.near[k, grow, :], 0, s)
    return y, grad


def compute_group(g, load, send, s):
    s.v[...] = load(0)
    inner_act = conv(0, g, s.v, True, s)
    s.act[...] = inner_act
    s.mixed[...] = load(1) * inner_act
    outer_act = conv(1, g, s.mixed, False, s)
    send(2, outer_act)
    s.x[...] = load(2)
    grad_mixed, grad_outer = corr(1, g, s.x, s.mixed, False, s)
    send(1, grad_mixed * s.act[...])
    s.x[...] = grad_mixed * load(1)
    grad_value, grad_inner = corr(0, g, s.x, s.v, True, s)
    send(0, grad_value)
    return jnp.where(lanes((G, T)) < F, grad_inner, grad_outer)


COMPUTE_SCRATCH = dict(
    basis_hi=((2, 2 * T, 2 * T), bf16),
    basis_lo=((2, 2 * T, 2 * T), bf16),
    feat_hi=((T, T), bf16),
    feat_lo=((T, T), bf16),
    flip=((T, T), bf16),
    gain=((2, CH, T), f32),
    weight=((2, CH, T), f32),
    window=((2, CH, T), f32),
    taps=((2, CH, T), f32),
    near=((2, CH, T), f32),
    far=((2, CH, T), f32),
    turn_re=((2, CH, T), f32),
    turn_im=((2, CH, T), f32),
    toep_hi=((2 * CH, T, T), bf16),
    toep_lo=((2 * CH, T, T), bf16),
    local=((ROWS // 2, 2 * T), f32),
    state=((2, ROWS // 2, 2 * T), f32),
    back=((ROWS // 2, 2 * T), f32),
    v=((ROWS, T), f32),
    mixed=((ROWS, T), f32),
    act=((ROWS, T), f32),
    x=((ROWS, T), f32),
    y=((ROWS, T), f32),
    lag=((G, T), f32),
)


def remote(src, dst, send, recv, **where):
    return pltpu.make_async_remote_copy(
        src_ref=src, dst_ref=dst, send_sem=send, recv_sem=recv, device_id=where, device_id_type=MESH
    )


def await_bytes(ref, sem):
    pltpu.make_async_copy(ref, ref, sem).wait()


def kernel(names, quarter, *refs):
    inputs, refs = refs[:4], refs[4:]
    small = refs[:3]
    outer_ref, inner_ref, grad_ref, refs = refs[3], refs[4], refs[5], refs[6:]
    s = SimpleNamespace(**dict(zip(names, refs)))
    me, mine = lax.axis_index("seq"), lax.axis_index("ch")
    mx, mz, my = lax.rem(me, 2), lax.rem(me // 2, 8), me // 16

    tables = (s.proj, s.decay, s.freq)

    def packing(i, g):
        if i >= 2:
            return pltpu.make_async_copy(inputs[i], (s.gate, s.cotangent)[i - 2], s.pack_sem.at[0, i])
        source = inputs[i].at[:, pl.ds(g * G, G), :]
        return pltpu.make_async_copy(source, s.leaves.at[g, :, i], s.pack_sem.at[g, i])

    for i, g in ((0, 0), (1, 0), (2, 0), (3, 0), (0, 1), (1, 1)):
        packing(i, g).start()
    for i in range(3):
        pltpu.make_async_copy(small[i], tables[i], s.table_sem.at[i]).start()
    barrier = pltpu.get_barrier_semaphore()

    def greet(j, _):
        pl.semaphore_signal(
            barrier, inc=1, device_id={"seq": lax.rem(me + j, N)}, device_id_type=MESH
        )
        return 0

    def layer(j):
        return dict(seq=lax.rem(j, 4) * 16 + mz * 2 + lax.rem(j // 4, 2), ch=j // 8)

    def greet_layer(j, _):
        spot = layer(lax.rem(mine * 8 + j, layer_size))
        pl.semaphore_signal(barrier, inc=1, device_id=spot, device_id_type=MESH)
        return 0

    layer_size = 8 * quarter
    lax.fori_loop(1, N, greet, 0, unroll=9)
    lax.fori_loop(8, layer_size, greet_layer, 0, unroll=8)
    pl.semaphore_wait(barrier, N - 1 + layer_size - 8)

    def push_all(source, target, send, recv):
        def push(j, _):
            p = lax.rem(me + j, N)
            remote(source.at[p], target.at[me], send, recv, seq=p).start()
            return 0

        lax.fori_loop(1, N, push, 0, unroll=9)
        pltpu.make_async_copy(source.at[me], target.at[me], recv).start()

    def push_in(g, k):
        sems = s.in_send.at[g, k], s.in_recv.at[g, k]
        if k == 0:
            push_all(s.leaves.at[g], s.came.at[g], *sems)
        else:
            push_all(s.leaves_outer.at[g], s.came_outer.at[g], *sems)

    def push_out(source, target, g, k):
        push_all(source.at[g], target.at[g], s.out_send.at[g, k], s.out_recv.at[g, k])

    packing(0, 0).wait()
    packing(1, 0).wait()
    push_in(0, 0)
    packing(2, 0).wait()
    packing(3, 0).wait()
    product, top = encode(s.gate[...].astype(f32) * s.cotangent[...].astype(f32))
    s.leaves_outer[0] = product[:, :G]
    s.leaves_outer[1] = product[:, G:]
    s.leaves_top[...] = to_lanes(top, 0)
    push_all(s.leaves_top, s.came_top, s.top_send.at[0], s.top_recv.at[0])
    push_in(0, 1)
    for i in range(3):
        pltpu.make_async_copy(small[i], tables[i], s.table_sem.at[i]).wait()
    prepare(me * CH, *tables, s)
    packing(0, 1).wait()
    packing(1, 1).wait()
    push_in(1, 0)
    push_in(1, 1)

    def share_column(g):
        spot = s.every.at[g, mx * 4 + my, mz]
        for j in range(1, 8):
            seq = my * 16 + lax.rem(mz + j, 8) * 2 + mx
            remote(spot, spot, s.share_send.at[0, g], s.share_recv.at[0, g], seq=seq).start()

    def share_layer(g):
        await_bytes(s.every.at[g, 0, pl.ds(0, 7)], s.share_recv.at[0, g])
        spot = s.every.at[g, mx * 4 + my]
        for j in range(1, 8):
            seq = layer(lax.rem(mx * 4 + my + j, 8))["seq"]
            remote(spot, spot, s.share_send.at[1, g], s.share_recv.at[1, g], seq=seq).start()

    for g in range(GROUPS):
        last = g == GROUPS - 1
        here = set()

        def load(i, g=g, here=here):
            if i == 2:
                if g == 0:
                    await_bytes(s.came_top, s.top_recv.at[0])
                await_bytes(s.came_outer.at[g], s.in_recv.at[g, 1])
                top = from_lanes(s.came_top[...], g * G, G)
                return decode(s.came_outer[g], top).reshape(ROWS, T)
            if not here:
                here.add(0)
                await_bytes(s.came.at[g], s.in_recv.at[g, 0])
            return s.came[g, :, i].reshape(ROWS, T).astype(f32)

        def send(i, val, g=g, last=last):
            if i == 2:
                s.goes_outer[g], top = encode(val.reshape(N, G, T))
                row = to_lanes(top, g * G)
                s.goes_top[...] = row + s.goes_top[...] if g else row
                push_out(s.goes_outer, s.back_outer, g, 0)
                if last:
                    push_all(s.goes_top, s.back_top, s.top_send.at[1], s.top_recv.at[1])
                return
            s.goes_inner[g, :, i] = val.astype(bf16).reshape(N, G, T)
            if i == 0 and not last:
                push_out(s.goes_inner, inner_ref, g, 1)

        s.every[g, mx * 4 + my, mz] = compute_group(g, load, send, s)
        share_column(g)
    share_layer(0)
    push_out(s.goes_inner, inner_ref, g, 1)
    share_layer(g)
    column = s.every[:, mx * 4 + my].reshape(2 * 8 * G, T)
    at = mine * 8 + mx * 4 + my
    s.square[at] = jnp.sum(column * column, axis=0, keepdims=True)

    def push_square(j, _):
        spot = s.square.at[at]
        where = layer(lax.rem(at + j, layer_size))
        remote(spot, spot, s.square_send, s.square_recv, **where).start()
        return 0

    lax.fori_loop(1, layer_size, push_square, 0)

    await_bytes(s.back_top, s.top_recv.at[1])
    for g in range(GROUPS):
        await_bytes(s.back_outer.at[g], s.out_recv.at[g, 0])
        rows = pl.ds(g * G, G)
        outer_act = decode(s.back_outer[g], from_lanes(s.back_top[...], g * G, G))
        outer_ref[:, rows, :] = (s.cotangent[:, rows, :].astype(f32) * outer_act).astype(bf16)

    await_bytes(s.square.at[pl.ds(0, layer_size - 1)], s.square_recv)
    total = jnp.sum(jnp.sum(s.square[...], axis=0), axis=1, keepdims=True)
    scale = lax.rsqrt(total / float(2 * F * CH * N * quarter) + 1e-06)
    for g in range(GROUPS):
        await_bytes(s.every.at[g, pl.ds(0, 7)], s.share_recv.at[1, g])
    for y in range(4):
        for z in range(8):
            for x in range(2):
                for g in range(GROUPS):
                    rows = pl.ds((y * 16 + z * 2 + x) * CH + g * G, G)
                    s.sorted[rows, :] = s.every[g, x * 4 + y, z] * scale
    for j in range(N * CH // T):
        grad_ref[:, pl.ds(j * T, T)] = s.sorted[pl.ds(j * T, T), :].T

    sent = pl.ds(0, N - 1)
    for way in (0, 1):
        await_bytes(s.back_top.at[sent], s.top_send.at[way])
    for g in range(GROUPS):
        await_bytes(inner_ref.at[g], s.out_recv.at[g, 1])
        await_bytes(s.came.at[g, sent], s.in_send.at[g, 0])
        await_bytes(s.came_outer.at[g, sent], s.in_send.at[g, 1])
        await_bytes(s.goes_outer.at[g, sent], s.out_send.at[g, 0])
        await_bytes(s.goes_inner.at[g, sent], s.out_send.at[g, 1])
        await_bytes(s.every.at[g, 0, pl.ds(0, 7)], s.share_send.at[0, g])
        await_bytes(s.every.at[g, pl.ds(0, 7)], s.share_send.at[1, g])
    await_bytes(s.square.at[pl.ds(0, layer_size - 1)], s.square_send)


def hand_over(outer_ref, inner_ref, grad_ref, value_out, inner_out, outer_out, grad_out, sems):
    copies = [pltpu.make_async_copy(grad_ref, grad_out, sems.at[6])]
    for g in range(GROUPS):
        rows = (slice(None), pl.ds(g * G, G), slice(None))
        for i, (source, target) in enumerate(
            (
                (inner_ref.at[g, :, 0], value_out),
                (inner_ref.at[g, :, 1], inner_out),
                (outer_ref.at[rows], outer_out),
            )
        ):
            copies.append(pltpu.make_async_copy(source, target.at[rows], sems.at[g * 3 + i]))
    for copy in copies:
        copy.start()
    for copy in copies:
        copy.wait()


def body(quarter, value_in, gate_inner, gate_outer, out_grad, filter_proj, decay, frequency):
    scratch = {name: pltpu.VMEM(*spec) for name, spec in COMPUTE_SCRATCH.items()}
    scratch |= dict(
        gate=pltpu.VMEM((N, CH, T), bf16),
        cotangent=pltpu.VMEM((N, CH, T), bf16),
        leaves=pltpu.VMEM((GROUPS, N, 2, G, T), bf16),
        came=pltpu.VMEM((GROUPS, N, 2, G, T), bf16),
        leaves_outer=pltpu.VMEM((GROUPS, N, G, T), bf16),
        came_outer=pltpu.VMEM((GROUPS, N, G, T), bf16),
        back_outer=pltpu.VMEM((GROUPS, N, G, T), bf16),
        leaves_top=pltpu.VMEM((N, 1, T), f32),
        came_top=pltpu.VMEM((N, 1, T), f32),
        goes_top=pltpu.VMEM((N, 1, T), f32),
        back_top=pltpu.VMEM((N, 1, T), f32),
        top_send=pltpu.SemaphoreType.DMA((2,)),
        top_recv=pltpu.SemaphoreType.DMA((2,)),
        goes_outer=pltpu.VMEM((GROUPS, N, G, T), bf16),
        goes_inner=pltpu.VMEM((GROUPS, N, 2, G, T), bf16),
        every=pltpu.VMEM((GROUPS, 8, 8, G, T), f32),
        sorted=pltpu.VMEM((N * CH, T), f32),
        square=pltpu.VMEM((8 * quarter, 1, T), f32),
        proj=pltpu.VMEM((2, F, filter_proj.shape[1]), bf16),
        decay=pltpu.VMEM(decay.shape, f32),
        freq=pltpu.VMEM((1, F), f32),
        table_sem=pltpu.SemaphoreType.DMA((3,)),
        pack_sem=pltpu.SemaphoreType.DMA((GROUPS, 4)),
        in_send=pltpu.SemaphoreType.DMA((GROUPS, 2)),
        in_recv=pltpu.SemaphoreType.DMA((GROUPS, 2)),
        out_send=pltpu.SemaphoreType.DMA((GROUPS, 2)),
        out_recv=pltpu.SemaphoreType.DMA((GROUPS, 2)),
        share_send=pltpu.SemaphoreType.DMA((2, GROUPS)),
        share_recv=pltpu.SemaphoreType.DMA((2, GROUPS)),
        square_send=pltpu.SemaphoreType.DMA,
        square_recv=pltpu.SemaphoreType.DMA,
    )
    local = jax.ShapeDtypeStruct((N, CH, T), bf16)
    grad = jax.ShapeDtypeStruct((T, N * CH), f32)
    anywhere, vmem = pl.BlockSpec(memory_space=pl.ANY), pl.BlockSpec(memory_space=pltpu.VMEM)
    hbm = pl.BlockSpec(memory_space=pltpu.HBM)
    results = pl.pallas_call(
        functools.partial(kernel, tuple(scratch), quarter),
        out_shape=(
            local,
            jax.ShapeDtypeStruct((GROUPS, N, 2, G, T), bf16),
            grad,
        ),
        in_specs=[hbm] * 7,
        out_specs=[vmem, anywhere, vmem],
        scratch_shapes=list(scratch.values()),
        compiler_params=pltpu.CompilerParams(
            collective_id=0, has_side_effects=True, vmem_limit_bytes=40 << 20
        ),
    )(
        *(
            pltpu.with_memory_space_constraint(x, pltpu.HBM)
            for x in (
                *(x.reshape(N, CH, T) for x in (value_in, gate_inner, gate_outer, out_grad)),
                jnp.transpose(filter_proj, (0, 2, 1)),
                decay,
                frequency.reshape(1, F),
            )
        )
    )
    grad_value, grad_inner, grad_outer, grads = pl.pallas_call(
        hand_over,
        out_shape=(local, local, local, grad),
        in_specs=[vmem] * 3,
        out_specs=[hbm] * 4,
        scratch_shapes=[pltpu.SemaphoreType.DMA((7,))],
    )(*(pltpu.with_memory_space_constraint(x, pltpu.VMEM) for x in results))
    filter_grad = jnp.transpose(grads.reshape(2, F, N * CH), (0, 2, 1))
    flat = tuple(x.reshape(N * CH, T) for x in (grad_value, grad_inner, grad_outer))
    return (*flat, filter_grad)


def solution(mesh):
    placed = (P("ch", "seq"),) * 4 + (P(None, "ch", None), P(None, "ch"), P())
    return jax.shard_map(
        functools.partial(body, mesh.shape["ch"]),
        mesh=mesh,
        in_specs=placed,
        out_specs=(P("ch", "seq"),) * 3 + (P(None, "ch", None),),
        check_vma=False,
    )
```

```python
import functools
from types import SimpleNamespace

import jax
import jax.numpy as jnp
from jax import lax
from jax.experimental import pallas as pl
from jax.experimental.pallas import tpu as pltpu
from jax.sharding import PartitionSpec as P

MESH = pl.DeviceIdType.MESH
f32, bf16 = jnp.float32, jnp.bfloat16
T = 128
N = 64
CH = 16
G = 8
GROUPS = CH // G
HALF = N // 2
ROWS = N * G
F = 64
NN = (((1,), (0,)), ((), ()))
NT = (((1,), (1,)), ((), ()))


def dg(a, b, dims=NN):
    return lax.dot_general(a, b, dims, preferred_element_type=f32)


def split(x):
    hi = x.astype(bf16)
    return hi, (x - hi.astype(f32)).astype(bf16)


def dot3(a, bh, bl, dims=NN):
    ah, al = split(a)
    return dg(ah, bh, dims) + (dg(al, bh, dims) + dg(ah, bl, dims))


def lanes(shape):
    return lax.broadcasted_iota(jnp.int32, shape, len(shape) - 1)


def rows_iota(shape):
    return lax.broadcasted_iota(jnp.int32, shape, 0)


def prepare(first, proj_ref, decay_ref, freq_ref, s):
    pick = lanes((CH, decay_ref.shape[1])) == rows_iota((CH, decay_ref.shape[1])) + first
    one_hot = pick.astype(f32).astype(bf16)
    low = lanes((T, T)) < F
    freq = jnp.concatenate([freq_ref[...], freq_ref[...]], 1)
    pos = rows_iota((T, T)).astype(f32)
    for which, num in ((0, (T - 1.0) - pos), (1, pos + 2.0)):
        angle = freq * num
        cos, sin = jnp.cos(angle), jnp.sin(angle)
        zero = jnp.zeros_like(cos)
        for half, keep in ((0, low), (1, jnp.logical_not(low))):
            for part, val in ((0, cos), (1, sin)):
                hi, lo = split(jnp.where(keep, val, zero))
                at = (which, pl.ds(half * T, T), pl.ds(part * T, T))
                s.basis_hi[at] = hi
                s.basis_lo[at] = lo
    fh, fl = split(jnp.sin(freq * (pos + 1.0)))
    s.feat_hi[...] = fh
    s.feat_lo[...] = fl
    s.flip[...] = (lanes((T, T)) + rows_iota((T, T)) == T - 1).astype(f32).astype(bf16)
    lane = lanes((CH, T)).astype(f32)
    turn = freq * float(T)
    turn_cos, turn_sin = jnp.cos(turn), jnp.sin(turn)
    for k in (0, 1):
        rate = jnp.sum(jnp.where(pick, decay_ref[pl.ds(k, 1), :], 0.0), axis=1, keepdims=True)
        rate = jnp.broadcast_to(rate, (CH, T))
        gain = jnp.sqrt(2.0 * rate)
        weights = dg(one_hot, proj_ref[k], NT)
        weights = jnp.concatenate([weights, weights], 1)
        window = gain * jnp.exp(-rate * lane)
        head = jnp.where(lanes((CH, T)) < F, weights, 0.0).astype(bf16)
        taps = (dg(head, fh, NT) + dg(head, fl, NT)) * window
        shrink = jnp.exp(-rate * float(T))
        for name, val in (
            ("gain", gain),
            ("weight", weights * gain),
            ("window", window),
            ("taps", taps),
            ("near", jnp.exp(-rate * ((T - 1.0) - lane))),
            ("far", jnp.exp(-rate * (lane + 1.0))),
            ("turn_re", shrink * turn_cos),
            ("turn_im", shrink * turn_sin),
        ):
            getattr(s, name)[k] = val
    ahead = lanes((T, T)) >= rows_iota((T, T))

    def toeplitz(i, _):
        k, d = i // CH, lax.rem(i, CH)
        row = jnp.broadcast_to(s.taps[k, pl.ds(d, 1), :], (T, T))
        mat = jnp.where(ahead, pltpu.roll(row, 0, 1, stride=1, stride_axis=0), 0.0)
        hi, lo = split(mat)
        s.toep_hi[i] = hi
        s.toep_lo[i] = lo
        return 0

    lax.fori_loop(0, 2 * CH, toeplitz, 0, unroll=4)


def encode(x):
    top = jnp.maximum(jnp.max(jnp.abs(x), axis=-1, keepdims=True), 1e-35)
    u = x / top
    q = u * u
    q = (q * q) * 2.0**60
    q = q * q
    return jnp.where(u < 0.0, -q, q).astype(bf16), top


def decode(y, top):
    y = y.astype(f32)
    root = jnp.sqrt(jnp.sqrt(jnp.sqrt(jnp.abs(y)) * 2.0**-60))
    root = jnp.where(y < 0.0, -root, jnp.where(y > 0.0, root, 0.0))
    return root * top


def to_lanes(top, first):
    n, m, _ = top.shape
    spot = lax.broadcasted_iota(jnp.int32, (n, m, T), 2) == first + lax.broadcasted_iota(
        jnp.int32, (n, m, T), 1
    )
    return jnp.sum(jnp.where(spot, jnp.broadcast_to(top, (n, m, T)), 0.0), axis=1, keepdims=True)


def from_lanes(row, first, m):
    n = row.shape[0]
    spot = lax.broadcasted_iota(jnp.int32, (n, m, T), 2) == first + lax.broadcasted_iota(
        jnp.int32, (n, m, T), 1
    )
    return jnp.sum(jnp.where(spot, jnp.broadcast_to(row, (n, m, T)), 0.0), axis=2, keepdims=True)


def of_channel(d):
    return pl.ds(d, N, stride=G)


def group_rows(g):
    return pl.ds(pl.multiple_of(g * G, G), G)


def over_chunks(x, row):
    n, m = x.shape[0] // G, x.shape[1]
    return (x.reshape(n, G, m) * row[None]).reshape(n * G, m)


def modal(x, weight, which, out, s):
    scaled = over_chunks(x, weight)
    scaled = jnp.concatenate([scaled[: ROWS // 2], scaled[ROWS // 2 :]], 1)
    out[...] = dot3(scaled, s.basis_hi[which], s.basis_lo[which])


def scan(src, dst, re, im, backward):
    def at(c):
        c = HALF - 1 - c if backward else c
        return pl.ds(pl.multiple_of(c * G, G), G)

    def step(store, c, carry):
        zr, zi = carry
        rows = at(c)
        if store:
            dst[rows, :T] = zr
            dst[rows, T:] = zi
        return (re * zr - im * zi) + src[rows, :T], (re * zi + im * zr) + src[rows, T:]

    zero = jnp.zeros((G, T), f32)
    end = lax.fori_loop(0, HALF, functools.partial(step, False), (zero, zero), unroll=HALF)
    late = lanes((G, T)) < F if backward else lanes((G, T)) >= F
    begin = tuple(jnp.where(late, pltpu.roll(x, F, 1), 0.0) for x in end)
    lax.fori_loop(0, HALF, functools.partial(step, True), begin, unroll=HALF)


def carried(state, weight, decay, which, s):
    z = jnp.concatenate([over_chunks(state[:, T:], weight), over_chunks(state[:, :T], weight)], 1)
    y = dot3(z, s.basis_hi[which], s.basis_lo[which], NT)
    return over_chunks(jnp.concatenate([y[:, :T], y[:, T:]], 0), decay)


def conv(k, g, x, exact, s):
    grow = group_rows(g)
    modal(x[...], s.near[k, grow, :], 0, s.local, s)
    scan(s.local, s.state.at[k], s.turn_re[k, grow, :], s.turn_im[k, grow, :], False)

    def channel(d, _):
        i = k * CH + g * G + d
        xh, xl = split(x[of_channel(d), :])
        y = dg(xh, s.toep_hi[i]) + dg(xh, s.toep_lo[i])
        if not exact:
            y = y + dg(xl, s.toep_hi[i])
        s.y[of_channel(d), :] = y
        return 0

    lax.fori_loop(0, G, channel, 0, unroll=8)
    return s.y[...] + carried(s.state[k], s.weight[k, grow, :], s.far[k, grow, :], 1, s)


def corr(k, g, x, signal, exact, s):
    grow = group_rows(g)
    modal(x[...], s.far[k, grow, :], 1, s.local, s)
    scan(s.local, s.back, s.turn_re[k, grow, :], s.turn_im[k, grow, :], True)

    def channel(d, _):
        i = k * CH + g * G + d
        xh, xl = split(x[of_channel(d), :])
        th = s.toep_hi[i]
        s.y[of_channel(d), :] = dg(xh, th, NT) + dg(xl, th, NT) + dg(xh, s.toep_lo[i], NT)
        vh, vl = split(signal[of_channel(d), :])
        if exact:
            left, right = [vh, vh], [xh, xl]
        else:
            left, right = [vh, vl, vh], [xh, xh, xl]
        turned = dg(s.flip[...], jnp.concatenate(left, 0), NT).astype(bf16)
        pairs = dg(turned, jnp.concatenate(right, 0))
        pairs = pltpu.roll(pairs, 1, 1, stride=1, stride_axis=0)
        pairs = jnp.where(lanes((T, T)) <= rows_iota((T, T)), pairs, 0.0)
        s.lag[pl.ds(d, 1), :] = jnp.sum(pairs, axis=0, keepdims=True)
        return 0

    lax.fori_loop(0, G, channel, 0, unroll=8)
    both = s.local[:, :T] * s.state[k, :, T:] + s.local[:, T:] * s.state[k, :, :T]
    both = jnp.sum(both.reshape(HALF, G, T), axis=0)
    both = both + pltpu.roll(both, F, 1)
    grad = dot3(s.lag[...] * s.window[k, grow, :], s.feat_hi[...], s.feat_lo[...])
    grad = grad + both * s.gain[k, grow, :]
    y = s.y[...] + carried(s.back, s.weight[k, grow, :], s.near[k, grow, :], 0, s)
    return y, grad


def compute_group(g, load, send, s):
    s.v[...] = load(0)
    inner_act = conv(0, g, s.v, True, s)
    s.act[...] = inner_act
    s.mixed[...] = load(1) * inner_act
    outer_act = conv(1, g, s.mixed, False, s)
    send(2, outer_act)
    s.x[...] = load(2)
    grad_mixed, grad_outer = corr(1, g, s.x, s.mixed, False, s)
    send(1, grad_mixed * s.act[...])
    s.x[...] = grad_mixed * load(1)
    grad_value, grad_inner = corr(0, g, s.x, s.v, True, s)
    send(0, grad_value)
    return jnp.where(lanes((G, T)) < F, grad_inner, grad_outer)


COMPUTE_SCRATCH = dict(
    basis_hi=((2, 2 * T, 2 * T), bf16),
    basis_lo=((2, 2 * T, 2 * T), bf16),
    feat_hi=((T, T), bf16),
    feat_lo=((T, T), bf16),
    flip=((T, T), bf16),
    gain=((2, CH, T), f32),
    weight=((2, CH, T), f32),
    window=((2, CH, T), f32),
    taps=((2, CH, T), f32),
    near=((2, CH, T), f32),
    far=((2, CH, T), f32),
    turn_re=((2, CH, T), f32),
    turn_im=((2, CH, T), f32),
    toep_hi=((2 * CH, T, T), bf16),
    toep_lo=((2 * CH, T, T), bf16),
    local=((ROWS // 2, 2 * T), f32),
    state=((2, ROWS // 2, 2 * T), f32),
    back=((ROWS // 2, 2 * T), f32),
    v=((ROWS, T), f32),
    mixed=((ROWS, T), f32),
    act=((ROWS, T), f32),
    x=((ROWS, T), f32),
    y=((ROWS, T), f32),
    lag=((G, T), f32),
)


def remote(src, dst, send, recv, **where):
    return pltpu.make_async_remote_copy(
        src_ref=src, dst_ref=dst, send_sem=send, recv_sem=recv, device_id=where, device_id_type=MESH
    )


def await_bytes(ref, sem):
    pltpu.make_async_copy(ref, ref, sem).wait()


def kernel(names, quarter, *refs):
    inputs, refs = refs[:4], refs[4:]
    small = refs[:3]
    outer_ref, inner_ref, grad_ref, refs = refs[3], refs[4], refs[5], refs[6:]
    s = SimpleNamespace(**dict(zip(names, refs)))
    me, mine = lax.axis_index("seq"), lax.axis_index("ch")
    mx, mz, my = lax.rem(me, 2), lax.rem(me // 2, 8), me // 16

    tables = (s.proj, s.decay, s.freq)

    def packing(i, g):
        if i >= 2:
            return pltpu.make_async_copy(inputs[i], (s.gate, s.cotangent)[i - 2], s.pack_sem.at[0, i])
        source = inputs[i].at[:, pl.ds(g * G, G), :]
        return pltpu.make_async_copy(source, s.leaves.at[g, :, i], s.pack_sem.at[g, i])

    packing(0, 0).start()
    packing(1, 0).start()
    barrier = pltpu.get_barrier_semaphore()

    def greet(j, _):
        pl.semaphore_signal(
            barrier, inc=1, device_id={"seq": lax.rem(me + j, N)}, device_id_type=MESH
        )
        return 0

    def layer(j):
        return dict(seq=lax.rem(j, 4) * 16 + mz * 2 + lax.rem(j // 4, 2), ch=j // 8)

    def greet_layer(j, _):
        spot = layer(lax.rem(mine * 8 + j, layer_size))
        pl.semaphore_signal(barrier, inc=1, device_id=spot, device_id_type=MESH)
        return 0

    layer_size = 8 * quarter
    lax.fori_loop(1, N, greet, 0, unroll=9)
    lax.fori_loop(8, layer_size, greet_layer, 0, unroll=8)
    for i, g in ((2, 0), (3, 0), (0, 1), (1, 1)):
        packing(i, g).start()
    for i in range(3):
        pltpu.make_async_copy(small[i], tables[i], s.table_sem.at[i]).start()
    pl.semaphore_wait(barrier, N - 1 + layer_size - 8)

    def push_all(source, target, send, recv):
        def push(j, _):
            p = lax.rem(me + j, N)
            remote(source.at[p], target.at[me], send, recv, seq=p).start()
            return 0

        lax.fori_loop(1, N, push, 0, unroll=9)
        pltpu.make_async_copy(source.at[me], target.at[me], recv).start()

    def push_in(g, k):
        sems = s.in_send.at[g, k], s.in_recv.at[g, k]
        if k == 0:
            push_all(s.leaves.at[g], s.came.at[g], *sems)
        else:
            push_all(s.leaves_outer.at[g], s.came_outer.at[g], *sems)

    def push_out(source, target, g, k):
        push_all(source.at[g], target.at[g], s.out_send.at[g, k], s.out_recv.at[g, k])

    packing(0, 0).wait()
    packing(1, 0).wait()
    push_in(0, 0)
    packing(2, 0).wait()
    packing(3, 0).wait()
    product, top = encode(s.gate[...].astype(f32) * s.cotangent[...].astype(f32))
    s.leaves_outer[0] = product[:, :G]
    s.leaves_outer[1] = product[:, G:]
    s.leaves_top[...] = to_lanes(top, 0)
    push_all(s.leaves_top, s.came_top, s.top_send.at[0], s.top_recv.at[0])
    push_in(0, 1)
    for i in range(3):
        pltpu.make_async_copy(small[i], tables[i], s.table_sem.at[i]).wait()
    prepare(me * CH, *tables, s)
    packing(0, 1).wait()
    packing(1, 1).wait()
    push_in(1, 0)
    push_in(1, 1)

    def share_column(g):
        spot = s.every.at[g, mx * 4 + my, mz]
        for j in range(1, 8):
            seq = my * 16 + lax.rem(mz + j, 8) * 2 + mx
            remote(spot, spot, s.share_send.at[0, g], s.share_recv.at[0, g], seq=seq).start()

    def share_layer(g):
        await_bytes(s.every.at[g, 0, pl.ds(0, 7)], s.share_recv.at[0, g])
        spot = s.every.at[g, mx * 4 + my]
        for j in range(1, 8):
            seq = layer(lax.rem(mx * 4 + my + j, 8))["seq"]
            remote(spot, spot, s.share_send.at[1, g], s.share_recv.at[1, g], seq=seq).start()

    for g in range(GROUPS):
        last = g == GROUPS - 1
        here = set()

        def load(i, g=g, here=here):
            if i == 2:
                if g == 0:
                    await_bytes(s.came_top, s.top_recv.at[0])
                await_bytes(s.came_outer.at[g], s.in_recv.at[g, 1])
                top = from_lanes(s.came_top[...], g * G, G)
                return decode(s.came_outer[g], top).reshape(ROWS, T)
            if not here:
                here.add(0)
                await_bytes(s.came.at[g], s.in_recv.at[g, 0])
            return s.came[g, :, i].reshape(ROWS, T).astype(f32)

        def send(i, val, g=g, last=last):
            if i == 2:
                s.goes_outer[g], top = encode(val.reshape(N, G, T))
                row = to_lanes(top, g * G)
                s.goes_top[...] = row + s.goes_top[...] if g else row
                push_out(s.goes_outer, s.back_outer, g, 0)
                if last:
                    push_all(s.goes_top, s.back_top, s.top_send.at[1], s.top_recv.at[1])
                return
            s.goes_inner[g, :, i] = val.astype(bf16).reshape(N, G, T)
            if i == 0 and not last:
                push_out(s.goes_inner, inner_ref, g, 1)

        s.every[g, mx * 4 + my, mz] = compute_group(g, load, send, s).astype(bf16)
        share_column(g)
    share_layer(0)
    push_out(s.goes_inner, inner_ref, g, 1)
    share_layer(g)
    column = s.every[:, mx * 4 + my].astype(f32).reshape(2 * 8 * G, T)
    at = mine * 8 + mx * 4 + my
    s.square[at] = jnp.sum(column * column, axis=0, keepdims=True)

    def push_square(j, _):
        spot = s.square.at[at]
        where = layer(lax.rem(at + j, layer_size))
        remote(spot, spot, s.square_send, s.square_recv, **where).start()
        return 0

    lax.fori_loop(1, layer_size, push_square, 0)

    await_bytes(s.back_top, s.top_recv.at[1])
    for g in range(GROUPS):
        await_bytes(s.back_outer.at[g], s.out_recv.at[g, 0])
        rows = pl.ds(g * G, G)
        outer_act = decode(s.back_outer[g], from_lanes(s.back_top[...], g * G, G))
        outer_ref[:, rows, :] = (s.cotangent[:, rows, :].astype(f32) * outer_act).astype(bf16)

    await_bytes(s.square.at[pl.ds(0, layer_size - 1)], s.square_recv)
    total = jnp.sum(jnp.sum(s.square[...], axis=0), axis=1, keepdims=True)
    scale = lax.rsqrt(total / float(2 * F * CH * N * quarter) + 1e-06)
    for g in range(GROUPS):
        await_bytes(s.every.at[g, pl.ds(0, 7)], s.share_recv.at[1, g])
    for y in range(4):
        for z in range(8):
            for x in range(2):
                for g in range(GROUPS):
                    rows = pl.ds((y * 16 + z * 2 + x) * CH + g * G, G)
                    s.sorted[rows, :] = s.every[g, x * 4 + y, z].astype(f32) * scale
    for j in range(N * CH // T):
        grad_ref[:, pl.ds(j * T, T)] = s.sorted[pl.ds(j * T, T), :].T

    sent = pl.ds(0, N - 1)
    for way in (0, 1):
        await_bytes(s.back_top.at[sent], s.top_send.at[way])
    for g in range(GROUPS):
        await_bytes(inner_ref.at[g], s.out_recv.at[g, 1])
        await_bytes(s.came.at[g, sent], s.in_send.at[g, 0])
        await_bytes(s.came_outer.at[g, sent], s.in_send.at[g, 1])
        await_bytes(s.goes_outer.at[g, sent], s.out_send.at[g, 0])
        await_bytes(s.goes_inner.at[g, sent], s.out_send.at[g, 1])
        await_bytes(s.every.at[g, 0, pl.ds(0, 7)], s.share_send.at[0, g])
        await_bytes(s.every.at[g, pl.ds(0, 7)], s.share_send.at[1, g])
    await_bytes(s.square.at[pl.ds(0, layer_size - 1)], s.square_send)


def hand_over(outer_ref, inner_ref, grad_ref, value_out, inner_out, outer_out, grad_out, sems):
    copies = [pltpu.make_async_copy(grad_ref, grad_out, sems.at[6])]
    for g in range(GROUPS):
        rows = (slice(None), pl.ds(g * G, G), slice(None))
        for i, (source, target) in enumerate(
            (
                (inner_ref.at[g, :, 0], value_out),
                (inner_ref.at[g, :, 1], inner_out),
                (outer_ref.at[rows], outer_out),
            )
        ):
            copies.append(pltpu.make_async_copy(source, target.at[rows], sems.at[g * 3 + i]))
    for copy in copies:
        copy.start()
    for copy in copies:
        copy.wait()


def body(quarter, value_in, gate_inner, gate_outer, out_grad, filter_proj, decay, frequency):
    scratch = {name: pltpu.VMEM(*spec) for name, spec in COMPUTE_SCRATCH.items()}
    scratch |= dict(
        gate=pltpu.VMEM((N, CH, T), bf16),
        cotangent=pltpu.VMEM((N, CH, T), bf16),
        leaves=pltpu.VMEM((GROUPS, N, 2, G, T), bf16),
        came=pltpu.VMEM((GROUPS, N, 2, G, T), bf16),
        leaves_outer=pltpu.VMEM((GROUPS, N, G, T), bf16),
        came_outer=pltpu.VMEM((GROUPS, N, G, T), bf16),
        back_outer=pltpu.VMEM((GROUPS, N, G, T), bf16),
        leaves_top=pltpu.VMEM((N, 1, T), f32),
        came_top=pltpu.VMEM((N, 1, T), f32),
        goes_top=pltpu.VMEM((N, 1, T), f32),
        back_top=pltpu.VMEM((N, 1, T), f32),
        top_send=pltpu.SemaphoreType.DMA((2,)),
        top_recv=pltpu.SemaphoreType.DMA((2,)),
        goes_outer=pltpu.VMEM((GROUPS, N, G, T), bf16),
        goes_inner=pltpu.VMEM((GROUPS, N, 2, G, T), bf16),
        every=pltpu.VMEM((GROUPS, 8, 8, G, T), bf16),
        sorted=pltpu.VMEM((N * CH, T), f32),
        square=pltpu.VMEM((8 * quarter, 1, T), f32),
        proj=pltpu.VMEM((2, F, filter_proj.shape[1]), bf16),
        decay=pltpu.VMEM(decay.shape, f32),
        freq=pltpu.VMEM((1, F), f32),
        table_sem=pltpu.SemaphoreType.DMA((3,)),
        pack_sem=pltpu.SemaphoreType.DMA((GROUPS, 4)),
        in_send=pltpu.SemaphoreType.DMA((GROUPS, 2)),
        in_recv=pltpu.SemaphoreType.DMA((GROUPS, 2)),
        out_send=pltpu.SemaphoreType.DMA((GROUPS, 2)),
        out_recv=pltpu.SemaphoreType.DMA((GROUPS, 2)),
        share_send=pltpu.SemaphoreType.DMA((2, GROUPS)),
        share_recv=pltpu.SemaphoreType.DMA((2, GROUPS)),
        square_send=pltpu.SemaphoreType.DMA,
        square_recv=pltpu.SemaphoreType.DMA,
    )
    local = jax.ShapeDtypeStruct((N, CH, T), bf16)
    grad = jax.ShapeDtypeStruct((T, N * CH), f32)
    anywhere, vmem = pl.BlockSpec(memory_space=pl.ANY), pl.BlockSpec(memory_space=pltpu.VMEM)
    hbm = pl.BlockSpec(memory_space=pltpu.HBM)
    results = pl.pallas_call(
        functools.partial(kernel, tuple(scratch), quarter),
        out_shape=(
            local,
            jax.ShapeDtypeStruct((GROUPS, N, 2, G, T), bf16),
            grad,
        ),
        in_specs=[hbm] * 7,
        out_specs=[vmem, anywhere, vmem],
        scratch_shapes=list(scratch.values()),
        compiler_params=pltpu.CompilerParams(
            collective_id=0, has_side_effects=True, vmem_limit_bytes=40 << 20
        ),
    )(
        *(
            pltpu.with_memory_space_constraint(x, pltpu.HBM)
            for x in (
                *(x.reshape(N, CH, T) for x in (value_in, gate_inner, gate_outer, out_grad)),
                jnp.transpose(filter_proj, (0, 2, 1)),
                decay,
                frequency.reshape(1, F),
            )
        )
    )
    grad_value, grad_inner, grad_outer, grads = pl.pallas_call(
        hand_over,
        out_shape=(local, local, local, grad),
        in_specs=[vmem] * 3,
        out_specs=[hbm] * 4,
        scratch_shapes=[pltpu.SemaphoreType.DMA((7,))],
    )(*(pltpu.with_memory_space_constraint(x, pltpu.VMEM) for x in results))
    filter_grad = jnp.transpose(grads.reshape(2, F, N * CH), (0, 2, 1))
    flat = tuple(x.reshape(N * CH, T) for x in (grad_value, grad_inner, grad_outer))
    return (*flat, filter_grad)


def solution(mesh):
    placed = (P("ch", "seq"),) * 4 + (P(None, "ch", None), P(None, "ch"), P())
    return jax.shard_map(
        functools.partial(body, mesh.shape["ch"]),
        mesh=mesh,
        in_specs=placed,
        out_specs=(P("ch", "seq"),) * 3 + (P(None, "ch", None),),
        check_vma=False,
    )
```

```python
import functools
from types import SimpleNamespace

import jax
import jax.numpy as jnp
from jax import lax
from jax.experimental import pallas as pl
from jax.experimental.pallas import tpu as pltpu
from jax.sharding import PartitionSpec as P

MESH = pl.DeviceIdType.MESH
f32, bf16 = jnp.float32, jnp.bfloat16
T = 128
N = 64
CH = 16
G = 8
GROUPS = CH // G
HALF = N // 2
ROWS = N * G
F = 64
NN = (((1,), (0,)), ((), ()))
NT = (((1,), (1,)), ((), ()))


def dg(a, b, dims=NN):
    return lax.dot_general(a, b, dims, preferred_element_type=f32)


def split(x):
    hi = x.astype(bf16)
    return hi, (x - hi.astype(f32)).astype(bf16)


def dot3(a, bh, bl, dims=NN):
    ah, al = split(a)
    return dg(ah, bh, dims) + (dg(al, bh, dims) + dg(ah, bl, dims))


def lanes(shape):
    return lax.broadcasted_iota(jnp.int32, shape, len(shape) - 1)


def rows_iota(shape):
    return lax.broadcasted_iota(jnp.int32, shape, 0)


def prepare(first, proj_ref, decay_ref, freq_ref, s):
    pick = lanes((CH, decay_ref.shape[1])) == rows_iota((CH, decay_ref.shape[1])) + first
    one_hot = pick.astype(f32).astype(bf16)
    low = lanes((T, T)) < F
    freq = jnp.concatenate([freq_ref[...], freq_ref[...]], 1)
    pos = rows_iota((T, T)).astype(f32)
    for which, num in ((0, (T - 1.0) - pos), (1, pos + 2.0)):
        angle = freq * num
        cos, sin = jnp.cos(angle), jnp.sin(angle)
        zero = jnp.zeros_like(cos)
        for half, keep in ((0, low), (1, jnp.logical_not(low))):
            for part, val in ((0, cos), (1, sin)):
                hi, lo = split(jnp.where(keep, val, zero))
                at = (which, pl.ds(half * T, T), pl.ds(part * T, T))
                s.basis_hi[at] = hi
                s.basis_lo[at] = lo
    fh, fl = split(jnp.sin(freq * (pos + 1.0)))
    s.feat_hi[...] = fh
    s.feat_lo[...] = fl
    s.flip[...] = (lanes((T, T)) + rows_iota((T, T)) == T - 1).astype(f32).astype(bf16)
    lane = lanes((CH, T)).astype(f32)
    turn = freq * float(T)
    turn_cos, turn_sin = jnp.cos(turn), jnp.sin(turn)
    for k in (0, 1):
        rate = jnp.sum(jnp.where(pick, decay_ref[pl.ds(k, 1), :], 0.0), axis=1, keepdims=True)
        rate = jnp.broadcast_to(rate, (CH, T))
        gain = jnp.sqrt(2.0 * rate)
        weights = dg(one_hot, proj_ref[k], NT)
        weights = jnp.concatenate([weights, weights], 1)
        window = gain * jnp.exp(-rate * lane)
        head = jnp.where(lanes((CH, T)) < F, weights, 0.0).astype(bf16)
        taps = (dg(head, fh, NT) + dg(head, fl, NT)) * window
        shrink = jnp.exp(-rate * float(T))
        for name, val in (
            ("gain", gain),
            ("weight", weights * gain),
            ("window", window),
            ("taps", taps),
            ("near", jnp.exp(-rate * ((T - 1.0) - lane))),
            ("far", jnp.exp(-rate * (lane + 1.0))),
            ("turn_re", shrink * turn_cos),
            ("turn_im", shrink * turn_sin),
        ):
            getattr(s, name)[k] = val
    ahead = lanes((T, T)) >= rows_iota((T, T))

    def toeplitz(i, _):
        k, d = i // CH, lax.rem(i, CH)
        row = jnp.broadcast_to(s.taps[k, pl.ds(d, 1), :], (T, T))
        mat = jnp.where(ahead, pltpu.roll(row, 0, 1, stride=1, stride_axis=0), 0.0)
        hi, lo = split(mat)
        s.toep_hi[i] = hi
        s.toep_lo[i] = lo
        return 0

    lax.fori_loop(0, 2 * CH, toeplitz, 0, unroll=4)


def encode(x):
    top = jnp.maximum(jnp.max(jnp.abs(x), axis=-1, keepdims=True), 1e-35)
    u = x / top
    q = u * u
    q = (q * q) * 2.0**60
    q = q * q
    return jnp.where(u < 0.0, -q, q).astype(bf16), top


def decode(y, top):
    y = y.astype(f32)
    root = jnp.sqrt(jnp.sqrt(jnp.sqrt(jnp.abs(y)) * 2.0**-60))
    root = jnp.where(y < 0.0, -root, jnp.where(y > 0.0, root, 0.0))
    return root * top


def to_lanes(top, first):
    n, m, _ = top.shape
    spot = lax.broadcasted_iota(jnp.int32, (n, m, T), 2) == first + lax.broadcasted_iota(
        jnp.int32, (n, m, T), 1
    )
    return jnp.sum(jnp.where(spot, jnp.broadcast_to(top, (n, m, T)), 0.0), axis=1, keepdims=True)


def from_lanes(row, first, m):
    n = row.shape[0]
    spot = lax.broadcasted_iota(jnp.int32, (n, m, T), 2) == first + lax.broadcasted_iota(
        jnp.int32, (n, m, T), 1
    )
    return jnp.sum(jnp.where(spot, jnp.broadcast_to(row, (n, m, T)), 0.0), axis=2, keepdims=True)


def of_channel(d):
    return pl.ds(d, N, stride=G)


def group_rows(g):
    return pl.ds(pl.multiple_of(g * G, G), G)


def over_chunks(x, row):
    n, m = x.shape[0] // G, x.shape[1]
    return (x.reshape(n, G, m) * row[None]).reshape(n * G, m)


def modal(x, weight, which, out, s):
    scaled = over_chunks(x, weight)
    scaled = jnp.concatenate([scaled[: ROWS // 2], scaled[ROWS // 2 :]], 1)
    out[...] = dot3(scaled, s.basis_hi[which], s.basis_lo[which])


def scan(src, dst, re, im, backward):
    def at(c):
        c = HALF - 1 - c if backward else c
        return pl.ds(pl.multiple_of(c * G, G), G)

    def step(store, c, carry):
        zr, zi = carry
        rows = at(c)
        if store:
            dst[rows, :T] = zr
            dst[rows, T:] = zi
        return (re * zr - im * zi) + src[rows, :T], (re * zi + im * zr) + src[rows, T:]

    zero = jnp.zeros((G, T), f32)
    end = lax.fori_loop(0, HALF, functools.partial(step, False), (zero, zero), unroll=HALF)
    late = lanes((G, T)) < F if backward else lanes((G, T)) >= F
    begin = tuple(jnp.where(late, pltpu.roll(x, F, 1), 0.0) for x in end)
    lax.fori_loop(0, HALF, functools.partial(step, True), begin, unroll=HALF)


def carried(state, weight, decay, which, s):
    z = jnp.concatenate([over_chunks(state[:, T:], weight), over_chunks(state[:, :T], weight)], 1)
    y = dot3(z, s.basis_hi[which], s.basis_lo[which], NT)
    return over_chunks(jnp.concatenate([y[:, :T], y[:, T:]], 0), decay)


def conv(k, g, x, exact, s):
    grow = group_rows(g)
    modal(x[...], s.near[k, grow, :], 0, s.local, s)
    scan(s.local, s.state.at[k], s.turn_re[k, grow, :], s.turn_im[k, grow, :], False)

    def channel(d, _):
        i = k * CH + g * G + d
        xh, xl = split(x[of_channel(d), :])
        y = dg(xh, s.toep_hi[i]) + dg(xh, s.toep_lo[i])
        if not exact:
            y = y + dg(xl, s.toep_hi[i])
        s.y[of_channel(d), :] = y
        return 0

    lax.fori_loop(0, G, channel, 0, unroll=8)
    return s.y[...] + carried(s.state[k], s.weight[k, grow, :], s.far[k, grow, :], 1, s)


def corr(k, g, x, signal, exact, s):
    grow = group_rows(g)
    modal(x[...], s.far[k, grow, :], 1, s.local, s)
    scan(s.local, s.back, s.turn_re[k, grow, :], s.turn_im[k, grow, :], True)

    def channel(d, _):
        i = k * CH + g * G + d
        xh, xl = split(x[of_channel(d), :])
        th = s.toep_hi[i]
        s.y[of_channel(d), :] = dg(xh, th, NT) + dg(xl, th, NT) + dg(xh, s.toep_lo[i], NT)
        vh, vl = split(signal[of_channel(d), :])
        if exact:
            left, right = [vh, vh], [xh, xl]
        else:
            left, right = [vh, vl, vh], [xh, xh, xl]
        turned = dg(s.flip[...], jnp.concatenate(left, 0), NT).astype(bf16)
        pairs = dg(turned, jnp.concatenate(right, 0))
        pairs = pltpu.roll(pairs, 1, 1, stride=1, stride_axis=0)
        pairs = jnp.where(lanes((T, T)) <= rows_iota((T, T)), pairs, 0.0)
        s.lag[pl.ds(d, 1), :] = jnp.sum(pairs, axis=0, keepdims=True)
        return 0

    lax.fori_loop(0, G, channel, 0, unroll=8)
    both = s.local[:, :T] * s.state[k, :, T:] + s.local[:, T:] * s.state[k, :, :T]
    both = jnp.sum(both.reshape(HALF, G, T), axis=0)
    both = both + pltpu.roll(both, F, 1)
    grad = dot3(s.lag[...] * s.window[k, grow, :], s.feat_hi[...], s.feat_lo[...])
    grad = grad + both * s.gain[k, grow, :]
    y = s.y[...] + carried(s.back, s.weight[k, grow, :], s.near[k, grow, :], 0, s)
    return y, grad


def compute_group(g, load, send, s):
    s.v[...] = load(0)
    inner_act = conv(0, g, s.v, True, s)
    s.act[...] = inner_act
    s.mixed[...] = load(1) * inner_act
    outer_act = conv(1, g, s.mixed, False, s)
    send(2, outer_act)
    s.x[...] = load(2)
    grad_mixed, grad_outer = corr(1, g, s.x, s.mixed, False, s)
    send(1, grad_mixed * s.act[...])
    s.x[...] = grad_mixed * load(1)
    grad_value, grad_inner = corr(0, g, s.x, s.v, True, s)
    send(0, grad_value)
    return jnp.where(lanes((G, T)) < F, grad_inner, grad_outer)


COMPUTE_SCRATCH = dict(
    basis_hi=((2, 2 * T, 2 * T), bf16),
    basis_lo=((2, 2 * T, 2 * T), bf16),
    feat_hi=((T, T), bf16),
    feat_lo=((T, T), bf16),
    flip=((T, T), bf16),
    gain=((2, CH, T), f32),
    weight=((2, CH, T), f32),
    window=((2, CH, T), f32),
    taps=((2, CH, T), f32),
    near=((2, CH, T), f32),
    far=((2, CH, T), f32),
    turn_re=((2, CH, T), f32),
    turn_im=((2, CH, T), f32),
    toep_hi=((2 * CH, T, T), bf16),
    toep_lo=((2 * CH, T, T), bf16),
    local=((ROWS // 2, 2 * T), f32),
    state=((2, ROWS // 2, 2 * T), f32),
    back=((ROWS // 2, 2 * T), f32),
    v=((ROWS, T), f32),
    mixed=((ROWS, T), f32),
    act=((ROWS, T), f32),
    x=((ROWS, T), f32),
    y=((ROWS, T), f32),
    lag=((G, T), f32),
)


def remote(src, dst, send, recv, **where):
    return pltpu.make_async_remote_copy(
        src_ref=src, dst_ref=dst, send_sem=send, recv_sem=recv, device_id=where, device_id_type=MESH
    )


def await_bytes(ref, sem):
    pltpu.make_async_copy(ref, ref, sem).wait()


def kernel(names, quarter, *refs):
    inputs, refs = refs[:4], refs[4:]
    small = refs[:3]
    outer_ref, inner_ref, grad_ref, refs = refs[3], refs[4], refs[5], refs[6:]
    s = SimpleNamespace(**dict(zip(names, refs)))
    me, mine = lax.axis_index("seq"), lax.axis_index("ch")
    mx, mz, my = lax.rem(me, 2), lax.rem(me // 2, 8), me // 16

    tables = (s.proj, s.decay, s.freq)

    def packing(i, g):
        if i >= 2:
            return pltpu.make_async_copy(inputs[i], (s.gate, s.cotangent)[i - 2], s.pack_sem.at[0, i])
        source = inputs[i].at[:, pl.ds(g * G, G), :]
        return pltpu.make_async_copy(source, s.leaves.at[g, :, i], s.pack_sem.at[g, i])

    packing(0, 0).start()
    packing(1, 0).start()
    barrier = pltpu.get_barrier_semaphore()

    def greet(j, _):
        pl.semaphore_signal(
            barrier, inc=1, device_id={"seq": lax.rem(me + j, N)}, device_id_type=MESH
        )
        return 0

    def layer(j):
        return dict(seq=lax.rem(j, 4) * 16 + mz * 2 + lax.rem(j // 4, 2), ch=j // 8)

    def greet_layer(j, _):
        spot = layer(lax.rem(mine * 8 + j, layer_size))
        pl.semaphore_signal(barrier, inc=1, device_id=spot, device_id_type=MESH)
        return 0

    layer_size = 8 * quarter
    lax.fori_loop(1, N, greet, 0, unroll=9)
    lax.fori_loop(8, layer_size, greet_layer, 0, unroll=8)
    for i, g in ((2, 0), (3, 0), (0, 1), (1, 1)):
        packing(i, g).start()
    for i in range(3):
        pltpu.make_async_copy(small[i], tables[i], s.table_sem.at[i]).start()
    pl.semaphore_wait(barrier, N - 1 + layer_size - 8)

    def push_all(source, target, send, recv):
        def push(j, _):
            p = lax.rem(me + j, N)
            remote(source.at[p], target.at[me], send, recv, seq=p).start()
            return 0

        lax.fori_loop(1, N, push, 0, unroll=9)
        pltpu.make_async_copy(source.at[me], target.at[me], recv).start()

    def push_in(g, k):
        sems = s.in_send.at[g, k], s.in_recv.at[g, k]
        if k == 0:
            push_all(s.leaves.at[g], s.came.at[g], *sems)
        else:
            push_all(s.leaves_outer.at[g], s.came_outer.at[g], *sems)

    def push_out(source, target, g, k):
        push_all(source.at[g], target.at[g], s.out_send.at[g, k], s.out_recv.at[g, k])

    packing(0, 0).wait()
    packing(1, 0).wait()
    push_in(0, 0)
    packing(2, 0).wait()
    packing(3, 0).wait()
    product, top = encode(s.gate[...].astype(f32) * s.cotangent[...].astype(f32))
    s.leaves_outer[0] = product[:, :G]
    s.leaves_outer[1] = product[:, G:]
    s.leaves_top[...] = to_lanes(top, 0)
    push_all(s.leaves_top, s.came_top, s.top_send.at[0], s.top_recv.at[0])
    push_in(0, 1)
    for i in range(3):
        pltpu.make_async_copy(small[i], tables[i], s.table_sem.at[i]).wait()
    prepare(me * CH, *tables, s)
    packing(0, 1).wait()
    packing(1, 1).wait()
    push_in(1, 0)
    push_in(1, 1)

    def share_column(g):
        spot = s.every.at[g, mx * 4 + my, mz]
        for j in range(1, 8):
            seq = my * 16 + lax.rem(mz + j, 8) * 2 + mx
            remote(spot, spot, s.share_send.at[0, g], s.share_recv.at[0, g], seq=seq).start()

    def share_layer(g):
        await_bytes(s.every.at[g, 0, pl.ds(0, 7)], s.share_recv.at[0, g])
        spot = s.every.at[g, mx * 4 + my]
        for j in range(1, 8):
            seq = layer(lax.rem(mx * 4 + my + j, 8))["seq"]
            remote(spot, spot, s.share_send.at[1, g], s.share_recv.at[1, g], seq=seq).start()

    for g in range(GROUPS):
        last = g == GROUPS - 1
        here = set()

        def load(i, g=g, here=here):
            if i == 2:
                if g == 0:
                    await_bytes(s.came_top, s.top_recv.at[0])
                await_bytes(s.came_outer.at[g], s.in_recv.at[g, 1])
                top = from_lanes(s.came_top[...], g * G, G)
                return decode(s.came_outer[g], top).reshape(ROWS, T)
            if not here:
                here.add(0)
                await_bytes(s.came.at[g], s.in_recv.at[g, 0])
            return s.came[g, :, i].reshape(ROWS, T).astype(f32)

        def send(i, val, g=g, last=last):
            if i == 2:
                s.goes_outer[g], top = encode(val.reshape(N, G, T))
                row = to_lanes(top, g * G)
                s.goes_top[...] = row + s.goes_top[...] if g else row
                push_out(s.goes_outer, s.back_outer, g, 0)
                if last:
                    push_all(s.goes_top, s.back_top, s.top_send.at[1], s.top_recv.at[1])
                return
            s.goes_inner[g, :, i] = val.astype(bf16).reshape(N, G, T)
            if i == 0 and not last:
                push_out(s.goes_inner, inner_ref, g, 1)

        s.every[g, mx * 4 + my, mz] = compute_group(g, load, send, s).astype(bf16)
        share_column(g)
    push_out(s.goes_inner, inner_ref, g, 1)
    share_layer(0)
    share_layer(g)
    column = s.every[:, mx * 4 + my].astype(f32).reshape(2 * 8 * G, T)
    at = mine * 8 + mx * 4 + my
    s.square[at] = jnp.sum(column * column, axis=0, keepdims=True)

    def push_square(j, _):
        spot = s.square.at[at]
        where = layer(lax.rem(at + j, layer_size))
        remote(spot, spot, s.square_send, s.square_recv, **where).start()
        return 0

    lax.fori_loop(1, layer_size, push_square, 0)

    await_bytes(s.back_top, s.top_recv.at[1])
    for g in range(GROUPS):
        await_bytes(s.back_outer.at[g], s.out_recv.at[g, 0])
        rows = pl.ds(g * G, G)
        outer_act = decode(s.back_outer[g], from_lanes(s.back_top[...], g * G, G))
        outer_ref[:, rows, :] = (s.cotangent[:, rows, :].astype(f32) * outer_act).astype(bf16)

    await_bytes(s.square.at[pl.ds(0, layer_size - 1)], s.square_recv)
    total = jnp.sum(jnp.sum(s.square[...], axis=0), axis=1, keepdims=True)
    scale = lax.rsqrt(total / float(2 * F * CH * N * quarter) + 1e-06)
    for g in range(GROUPS):
        await_bytes(s.every.at[g, pl.ds(0, 7)], s.share_recv.at[1, g])
    for y in range(4):
        for z in range(8):
            for x in range(2):
                for g in range(GROUPS):
                    rows = pl.ds((y * 16 + z * 2 + x) * CH + g * G, G)
                    s.sorted[rows, :] = s.every[g, x * 4 + y, z].astype(f32) * scale
    for j in range(N * CH // T):
        grad_ref[:, pl.ds(j * T, T)] = s.sorted[pl.ds(j * T, T), :].T

    sent = pl.ds(0, N - 1)
    for way in (0, 1):
        await_bytes(s.back_top.at[sent], s.top_send.at[way])
    for g in range(GROUPS):
        await_bytes(inner_ref.at[g], s.out_recv.at[g, 1])
        await_bytes(s.came.at[g, sent], s.in_send.at[g, 0])
        await_bytes(s.came_outer.at[g, sent], s.in_send.at[g, 1])
        await_bytes(s.goes_outer.at[g, sent], s.out_send.at[g, 0])
        await_bytes(s.goes_inner.at[g, sent], s.out_send.at[g, 1])
        await_bytes(s.every.at[g, 0, pl.ds(0, 7)], s.share_send.at[0, g])
        await_bytes(s.every.at[g, pl.ds(0, 7)], s.share_send.at[1, g])
    await_bytes(s.square.at[pl.ds(0, layer_size - 1)], s.square_send)


def hand_over(outer_ref, inner_ref, grad_ref, value_out, inner_out, outer_out, grad_out, sems):
    copies = [pltpu.make_async_copy(grad_ref, grad_out, sems.at[6])]
    for g in range(GROUPS):
        rows = (slice(None), pl.ds(g * G, G), slice(None))
        for i, (source, target) in enumerate(
            (
                (inner_ref.at[g, :, 0], value_out),
                (inner_ref.at[g, :, 1], inner_out),
                (outer_ref.at[rows], outer_out),
            )
        ):
            copies.append(pltpu.make_async_copy(source, target.at[rows], sems.at[g * 3 + i]))
    for copy in copies:
        copy.start()
    for copy in copies:
        copy.wait()


def body(quarter, value_in, gate_inner, gate_outer, out_grad, filter_proj, decay, frequency):
    scratch = {name: pltpu.VMEM(*spec) for name, spec in COMPUTE_SCRATCH.items()}
    scratch |= dict(
        gate=pltpu.VMEM((N, CH, T), bf16),
        cotangent=pltpu.VMEM((N, CH, T), bf16),
        leaves=pltpu.VMEM((GROUPS, N, 2, G, T), bf16),
        came=pltpu.VMEM((GROUPS, N, 2, G, T), bf16),
        leaves_outer=pltpu.VMEM((GROUPS, N, G, T), bf16),
        came_outer=pltpu.VMEM((GROUPS, N, G, T), bf16),
        back_outer=pltpu.VMEM((GROUPS, N, G, T), bf16),
        leaves_top=pltpu.VMEM((N, 1, T), f32),
        came_top=pltpu.VMEM((N, 1, T), f32),
        goes_top=pltpu.VMEM((N, 1, T), f32),
        back_top=pltpu.VMEM((N, 1, T), f32),
        top_send=pltpu.SemaphoreType.DMA((2,)),
        top_recv=pltpu.SemaphoreType.DMA((2,)),
        goes_outer=pltpu.VMEM((GROUPS, N, G, T), bf16),
        goes_inner=pltpu.VMEM((GROUPS, N, 2, G, T), bf16),
        every=pltpu.VMEM((GROUPS, 8, 8, G, T), bf16),
        sorted=pltpu.VMEM((N * CH, T), f32),
        square=pltpu.VMEM((8 * quarter, 1, T), f32),
        proj=pltpu.VMEM((2, F, filter_proj.shape[1]), bf16),
        decay=pltpu.VMEM(decay.shape, f32),
        freq=pltpu.VMEM((1, F), f32),
        table_sem=pltpu.SemaphoreType.DMA((3,)),
        pack_sem=pltpu.SemaphoreType.DMA((GROUPS, 4)),
        in_send=pltpu.SemaphoreType.DMA((GROUPS, 2)),
        in_recv=pltpu.SemaphoreType.DMA((GROUPS, 2)),
        out_send=pltpu.SemaphoreType.DMA((GROUPS, 2)),
        out_recv=pltpu.SemaphoreType.DMA((GROUPS, 2)),
        share_send=pltpu.SemaphoreType.DMA((2, GROUPS)),
        share_recv=pltpu.SemaphoreType.DMA((2, GROUPS)),
        square_send=pltpu.SemaphoreType.DMA,
        square_recv=pltpu.SemaphoreType.DMA,
    )
    local = jax.ShapeDtypeStruct((N, CH, T), bf16)
    grad = jax.ShapeDtypeStruct((T, N * CH), f32)
    anywhere, vmem = pl.BlockSpec(memory_space=pl.ANY), pl.BlockSpec(memory_space=pltpu.VMEM)
    hbm = pl.BlockSpec(memory_space=pltpu.HBM)
    results = pl.pallas_call(
        functools.partial(kernel, tuple(scratch), quarter),
        out_shape=(
            local,
            jax.ShapeDtypeStruct((GROUPS, N, 2, G, T), bf16),
            grad,
        ),
        in_specs=[hbm] * 7,
        out_specs=[vmem, anywhere, vmem],
        scratch_shapes=list(scratch.values()),
        compiler_params=pltpu.CompilerParams(
            collective_id=0, has_side_effects=True, vmem_limit_bytes=40 << 20
        ),
    )(
        *(
            pltpu.with_memory_space_constraint(x, pltpu.HBM)
            for x in (
                *(x.reshape(N, CH, T) for x in (value_in, gate_inner, gate_outer, out_grad)),
                jnp.transpose(filter_proj, (0, 2, 1)),
                decay,
                frequency.reshape(1, F),
            )
        )
    )
    grad_value, grad_inner, grad_outer, grads = pl.pallas_call(
        hand_over,
        out_shape=(local, local, local, grad),
        in_specs=[vmem] * 3,
        out_specs=[hbm] * 4,
        scratch_shapes=[pltpu.SemaphoreType.DMA((7,))],
    )(*(pltpu.with_memory_space_constraint(x, pltpu.VMEM) for x in results))
    filter_grad = jnp.transpose(grads.reshape(2, F, N * CH), (0, 2, 1))
    flat = tuple(x.reshape(N * CH, T) for x in (grad_value, grad_inner, grad_outer))
    return (*flat, filter_grad)


def solution(mesh):
    placed = (P("ch", "seq"),) * 4 + (P(None, "ch", None), P(None, "ch"), P())
    return jax.shard_map(
        functools.partial(body, mesh.shape["ch"]),
        mesh=mesh,
        in_specs=placed,
        out_specs=(P("ch", "seq"),) * 3 + (P(None, "ch", None),),
        check_vma=False,
    )
```
